32 devices in a mesh: gx: 8 (over y, x, core), gy: 4 (over z).
Axes of the slice: x: 2, y: 2, z: 4, core: 2. Of those that a mesh axis runs over, the one named last changes fastest.
Arguments:
- pressure: float32 [128, 256, 512], P('gx', 'gy'), may hold values from -3 to 3
- permeability: float32 [128, 256, 512], P('gx', 'gy'), may hold values from 0.1 to 1
- kernel: float32 [2, 1536, 1536], P(None, 'gx', 'gy'), may hold values from -1.2247449 to 1.2247449
- slip_rate: float32 [1536], P(('gx', 'gy')), may hold values from 0.1 to 1
- aging_state: float32 [1536], P(('gx', 'gy')), may hold values from 0.5 to 5
- normal_stress: float32 [1536], P(('gx', 'gy')), may hold values from 50 to 80
- shear_stress: float32 [1536], P(('gx', 'gy')), may hold values from 33 to 45
- direct_effect: float32 [1536], P(('gx', 'gy')), may hold values from 0.01 to 0.02
- evolution_effect: float32 [1536], P(('gx', 'gy')), may hold values from 0.01 to 0.03
- slip_distance: float32 [1536], P(('gx', 'gy')), may hold values from 0.2 to 1
- tri_owner: int32 [1536, 1], P(('gx', 'gy')), may hold values from 0 to 7; in each aligned block of 48 rows (0 to 47, 48 to 95, ...) at most 12 rows name the same one
- tri_cell: int32 [1536], P(('gx', 'gy')), may hold values from 0 to 524287
Outputs:
- pressure_next: float32 [128, 256, 512], P('gx', 'gy')
- state_next: float32 [1536], P(('gx', 'gy'))
- log_rate: float32 [1536], P(('gx', 'gy'))
The draws below stay inside these ranges and needn't reach their ends.
Inputs may be any that keep to these rules, and one draw needn't show every extreme that they name: `tri_owner`: at most 12 of the 48 triangles of one device name one owner, and in every draw some owner is named by exactly 12 triangles of some device.
All inputs are finite; a program needn't handle non-finite values.
Results may differ from the reference program's by a relative error of at most 0.000092.
Values sent between devices are 32-bit elements; how exact they have to be, the bound alone decides.
A program may use at most 64 MiB of HBM per device.

```python
import math
import jax
import jax.numpy as jnp
import numpy as np
from jax import lax

CX = 16
CY = 64
NZ = 512
SWEEPS = 3
TRI_DEV = 48
NTRI = 1536
CAP = 12
NX = 128
NY = 256
N_GX = 8
N_GY = 4


def set_ends(values, key, least, top_value):
    spot = [jax.random.randint(jax.random.fold_in(key, axis), (), 0, length) for axis, length in enumerate(values.shape)]
    main_axis = values.shape.index(max(values.shape))
    beside = spot[:main_axis] + [(spot[main_axis] + 1) % values.shape[main_axis]] + spot[main_axis + 1:]
    return values.at[tuple(spot)].set(least).at[tuple(beside)].set(top_value)


def level_of(rng, dims, pieces, smallest, top_value):
    def one(position, shards_of):
        heights = jax.random.uniform(jax.random.fold_in(jax.random.fold_in(rng, 6), position), (shards_of,), jnp.float32, smallest / len(pieces), top_value / len(pieces))
        return jnp.repeat(jnp.exp(heights), dims[position] // shards_of).reshape((-1,) + (1,) * (len(dims) - position - 1))

    level = one(*pieces[0])
    for cut in pieces[1:]:
        level = level * one(*cut)
    return level


def routed_block(rng, own, number, rows, amount, top, limit, skew):
    sequence = jax.random.permutation(rng, amount)
    packed, common = shares(amount, rows * top, limit, skew, True), shares(amount, rows * top, limit, skew, False)
    places = jnp.arange(amount)

    def named(lengths, offset_by):
        used = int((lengths > 0).sum())
        fixed = max(1, used // 4)
        passed = fixed + (places - fixed + offset_by * (used - fixed)) % max(1, amount - fixed)
        return jnp.zeros((amount,), jnp.int32).at[sequence[jnp.where(places < fixed, places, passed)]].set(jnp.asarray(lengths, jnp.int32))

    lengths = jnp.where(number % 4 == 0, named(packed, number // 4), named(common, number - number // 4 - 1))
    mixed = jax.random.permutation(jax.random.fold_in(own, 3), amount)
    source_of, receiver = mixed[0:amount // 2 * 2:2], mixed[1:amount // 2 * 2:2]
    slack = jnp.minimum(lengths[source_of] - 1, limit - lengths[receiver]) // 2
    slack = jnp.where((source_of == sequence[0]) | (receiver == sequence[0]) | (lengths[receiver] == 0), 0, jnp.maximum(slack, 0))
    passed = jax.random.randint(jax.random.fold_in(own, 4), (amount // 2,), 0, 1 << 20) % (slack + 1)
    lengths = lengths.at[source_of].add(-passed).at[receiver].add(passed)
    labels = jnp.searchsorted(jnp.cumsum(lengths), jnp.arange(rows * top), side="right").astype(jnp.int32)
    table = labels.reshape(top, rows).T
    table = table[jax.random.permutation(jax.random.fold_in(own, 1), rows)]
    offset_by = jax.random.randint(jax.random.fold_in(own, 2), (rows, 1), 0, top)
    return jnp.take_along_axis(table, (jnp.arange(top)[None, :] + offset_by) % top, axis=1)


def shares(count, total, bound, skew, full):
    loads = [(1 << 20) // math.isqrt(grade ** skew) + 1 for grade in range(1, count + 1)]
    largest = bound if full else min(bound, max(-(-total // count), total * loads[0] // sum(loads)))
    least = 1 if total - largest >= count - 1 else 0
    counts, spare = [largest] + [least] * (count - 1), total - largest - least * (count - 1)
    while spare > 0:
        candidates = [i for i in range(1, count) if counts[i] < largest] or [i for i in range(1, count) if counts[i] < bound]
        whole, left = sum([loads[i] for i in candidates]), spare
        for i in candidates:
            more = min(bound - counts[i], max(1, left * loads[i] // whole), spare)
            counts[i] = counts[i] + more
            spare = spare - more
    return np.array(counts)


def scatter_about(rng, shape, spread, most, pieces=(), held_as=jnp.bfloat16):
    array = spread * jax.random.normal(rng, shape, jnp.float32)
    if pieces:
        array = array * level_of(rng, shape, pieces, -0.22, 0.18)
    return jnp.clip(array, -most, most).astype(held_as)


def setup_inputs(seed: int = 0) -> dict:
    splits = jax.random.split(jax.random.key(seed), 13)
    pressure = scatter_about(splits[0], (NX, NY, NZ), 1.0, 3.0, ((0, 8), (1, 4)), jnp.float32)
    permeability = jnp.clip(jnp.exp(math.log(1.0) - 2.3025851 * jax.random.uniform(splits[1], (NX, NY, NZ), jnp.float32) ** level_of(splits[1], (NX, NY, NZ), ((0, 8), (1, 4)), -0.2, 0.2)), 0.1, 1.0)
    kernel = scatter_about(splits[2], (2, NTRI, NTRI), (8.0 / NTRI ** 0.5), 1.2247449, ((1, 8), (2, 4)), jnp.float32)
    slip_rate = jnp.clip(jnp.exp(math.log(1.0) - 2.3025851 * jax.random.uniform(splits[3], (NTRI,), jnp.float32) ** level_of(splits[3], (NTRI,), ((0, 32),), -0.2, 0.2)), 0.1, 1.0)
    aging_state = jnp.clip(jnp.exp(math.log(5.0) - 2.3025851 * jax.random.uniform(splits[4], (NTRI,), jnp.float32) ** level_of(splits[4], (NTRI,), ((0, 32),), -0.2, 0.2)), 0.5, 5.0)
    normal_stress = jnp.clip(50.0 + 30.0 * jax.random.uniform(splits[5], (NTRI,), jnp.float32) ** level_of(splits[5], (NTRI,), ((0, 32),), -0.2, 0.2), 50.0, 80.0)
    shear_stress = jnp.clip(33.0 + 12.0 * jax.random.uniform(splits[6], (NTRI,), jnp.float32) ** level_of(splits[6], (NTRI,), ((0, 32),), -0.2, 0.2), 33.0, 45.0)
    direct_effect = jnp.clip(jnp.exp(math.log(0.02) - 0.6931472 * jax.random.uniform(splits[7], (NTRI,), jnp.float32) ** level_of(splits[7], (NTRI,), ((0, 32),), -0.2, 0.2)), 0.01, 0.02)
    evolution_effect = jnp.clip(jnp.exp(math.log(0.03) - 1.0986123 * jax.random.uniform(splits[8], (NTRI,), jnp.float32) ** level_of(splits[8], (NTRI,), ((0, 32),), -0.2, 0.2)), 0.01, 0.03)
    slip_distance = jnp.clip(jnp.exp(math.log(1.0) - 1.609438 * jax.random.uniform(splits[9], (NTRI,), jnp.float32) ** level_of(splits[9], (NTRI,), ((0, 32),), -0.2, 0.2)), 0.2, 1.0)
    tri_owner_keys = jax.random.split(jax.random.fold_in(splits[10], 1), NTRI // TRI_DEV)
    tri_owner_turns = jax.random.permutation(jax.random.fold_in(splits[10], 3), NTRI // TRI_DEV)
    tri_owner = jax.vmap(lambda own, number: routed_block(jax.random.fold_in(splits[10], 2), own, number, TRI_DEV, N_GX, 1, CAP, 2))(tri_owner_keys, tri_owner_turns).reshape((NTRI, 1))
    tri_cell = set_ends(jax.random.randint(splits[11], (NTRI,), 0, CX * CY * NZ), jax.random.fold_in(splits[11], 1), 0, (CX * CY * NZ) - 1).astype(jnp.int32)
    return {"pressure": pressure, "permeability": permeability, "kernel": kernel, "slip_rate": slip_rate, "aging_state": aging_state, "normal_stress": normal_stress, "shear_stress": shear_stress, "direct_effect": direct_effect, "evolution_effect": evolution_effect, "slip_distance": slip_distance, "tri_owner": tri_owner, "tri_cell": tri_cell}


conductance = 0.15
step_time = 1.0
heal_time = 0.5
friction_ref = 0.6
neighbours = ((1, 0, 0), (-1, 0, 0), (0, 1, 0), (0, -1, 0), (0, 0, 1), (0, 0, -1))

def shifted(values, step_x, step_y, step_z):
    return values[1 + step_x:values.shape[0] - 1 + step_x, 1 + step_y:values.shape[1] - 1 + step_y, 1 + step_z:values.shape[2] - 1 + step_z]

def explicit_step(padded_p, padded_k):
    full_p = jnp.pad(padded_p, ((0, 0), (0, 0), (1, 1)))
    full_k = jnp.pad(padded_k, ((0, 0), (0, 0), (1, 1)))
    centre_p = shifted(full_p, 0, 0, 0)
    centre_k = shifted(full_k, 0, 0, 0)
    flux = jnp.zeros_like(centre_p)
    for offset in neighbours:
        other_p = shifted(full_p, offset[0], offset[1], offset[2])
        other_k = shifted(full_k, offset[0], offset[1], offset[2])
        flux = flux + jnp.sqrt(centre_k * other_k) * (other_p - centre_p)
    return centre_p + conductance * flux

def reference(pressure, permeability, kernel, slip_rate, aging_state, normal_stress, shear_stress, direct_effect, evolution_effect, slip_distance, tri_owner, tri_cell):
    padded_k = jnp.pad(permeability, ((1, 1), (1, 1), (0, 0)))
    pressure_field = pressure
    for repeat in range(SWEEPS):
        pressure_field = explicit_step(jnp.pad(pressure_field, ((1, 1), (1, 1), (0, 0))), padded_k)
    triangles = jnp.arange(NTRI, dtype=jnp.int32)
    column_dev = triangles // TRI_DEV % N_GY
    owners = tri_owner[:, 0].astype(jnp.int32)
    pos_x = owners * CX + tri_cell // (CY * NZ)
    pos_y = column_dev * CY + tri_cell // NZ % CY
    pos_z = tri_cell % NZ
    fault_pressure = pressure_field[pos_x, pos_y, pos_z]
    rates = jnp.dot(kernel.reshape(2 * NTRI, NTRI), slip_rate, precision=lax.Precision.HIGHEST).reshape(2, NTRI)
    shear = shear_stress + step_time * rates[0]
    effective = normal_stress + step_time * rates[1] - fault_pressure
    ratio = slip_distance / slip_rate
    state_next = ratio + (aging_state - ratio) * jnp.exp(-heal_time / ratio)
    log_rate = (shear / effective - friction_ref - evolution_effect * jnp.log(state_next / slip_distance)) / direct_effect
    return (pressure_field, state_next, log_rate)
```

```python
import functools

import jax
import jax.numpy as jnp
from jax import lax
from jax.experimental import pallas as pl
from jax.experimental.pallas import tpu as pltpu
from jax.sharding import PartitionSpec as P

SWEEPS = 3
LANES = 128
CHUNK = 16
MESH = pl.DeviceIdType.MESH

conductance = 0.15
step_time = 1.0
heal_time = 0.5
friction_ref = 0.6


def step_kernel(
    dims,
    p_hbm,
    k_hbm,
    g_hbm,
    slip_hbm,
    aging_hbm,
    normal_hbm,
    shear_hbm,
    direct_hbm,
    evolution_hbm,
    distance_hbm,
    owner_hbm,
    cell_hbm,
    out_v,
    state_ref,
    log_ref,
    p_in,
    k_in,
    g_in,
    vec_f,
    vec_i,
    root,
    u_a,
    u_b,
    coef_a,
    coef_c,
    inv,
    first_x,
    later_x_send,
    later_x,
    first_y_send,
    first_y,
    later_y_send,
    later_y,
    slip_send,
    slip_part,
    slip_recv,
    req_send,
    req_recv,
    req_smem,
    part_send,
    part_recv,
    ans_pick,
    ans_send,
    ans_recv,
    load_sem,
    vec_sem,
    fx_send,
    fx_recv,
    lx_send,
    lx_recv,
    y_send,
    y_recv,
    gather_ssem,
    gather_rsem,
    slip_ssem,
    slip_rsem,
    req_ssem,
    req_rsem,
    part_ssem,
    part_rsem,
    ans_ssem,
    ans_rsem,
):
    n_gx, n_gy, cx, cy, nz, tri, rows, cols, cap, cap_pad = dims
    nb = nz // LANES
    yp = cy + 8
    n_ch = cy // CHUNK
    edges = sorted({0, n_ch - 1})
    middles = [c for c in range(n_ch) if c not in edges]
    gx, gy = lax.axis_index("gx"), lax.axis_index("gy")
    lane = lax.broadcasted_iota(jnp.int32, (1, LANES), 1)

    smalls = (
        (owner_hbm, vec_i.at[0]),
        (cell_hbm, vec_i.at[1]),
        (slip_hbm, vec_f.at[0]),
        (aging_hbm, vec_f.at[1]),
        (normal_hbm, vec_f.at[2]),
        (shear_hbm, vec_f.at[3]),
        (direct_hbm, vec_f.at[4]),
        (evolution_hbm, vec_f.at[5]),
        (distance_hbm, vec_f.at[6]),
    )
    loads = [pltpu.make_async_copy(s, d, vec_sem.at[i]) for i, (s, d) in enumerate(smalls)]
    load_k = pltpu.make_async_copy(k_hbm, k_in, load_sem.at[0])
    load_p = pltpu.make_async_copy(p_hbm, p_in, load_sem.at[1])
    load_g = pltpu.make_async_copy(g_hbm, g_in, load_sem.at[2])

    barrier = pltpu.get_barrier_semaphore()

    def greet(x, y):
        pl.semaphore_signal(barrier, inc=1, device_id={"gx": x, "gy": y}, device_id_type=MESH)

    for off in range(1, n_gx):
        greet((gx + off) % n_gx, gy)
    for off in range(1, n_gy):
        greet(gx, (gy + off) % n_gy)
    for copy in loads[:3]:
        copy.start()
    load_k.start()
    load_p.start()
    load_g.start()
    for copy in loads[3:]:
        copy.start()

    zero = jnp.zeros((8, LANES), jnp.float32)
    n_col = (cx + 2) * nb
    for ref in (root, u_a, u_b):
        for c in range(nb, n_col - nb + 1):
            ref[c * yp : c * yp + 8, :] = zero
        ref[0 : nb * yp, :] = jnp.zeros((nb * yp, LANES), jnp.float32)
        ref[(cx + 1) * nb * yp : (cx + 2) * nb * yp + 8, :] = jnp.zeros(
            (nb * yp + 8, LANES), jnp.float32
        )

    for copy in loads[:3]:
        copy.wait()
    slip_send[...] = jnp.zeros_like(slip_send)
    slip_send[0, :, :tri] = vec_f[0]

    owner_row = vec_i[0]
    cell_row = vec_i[1]
    t_row = lax.broadcasted_iota(jnp.int32, (tri, tri), 1)
    t_col = lax.broadcasted_iota(jnp.int32, (tri, tri), 0)
    eye = t_row == t_col
    owner_wide = jnp.broadcast_to(owner_row, (tri, tri))
    owner_col = jnp.sum(jnp.where(eye, owner_wide, 0), axis=1, keepdims=True)
    cell_col = jnp.sum(
        jnp.where(eye, jnp.broadcast_to(cell_row, (tri, tri)), 0), axis=1, keepdims=True
    )
    same = owner_col == owner_wide
    one_below = jnp.where(same & (t_row < t_col), 1, 0)
    rank_col = jnp.sum(one_below, axis=1, keepdims=True)
    slot_col = owner_col * cap + rank_col
    width = req_send.shape[-1]
    slot_lane = lax.broadcasted_iota(jnp.int32, (tri, width), 1)
    req_send[0] = jnp.sum(jnp.where(slot_col == slot_lane, cell_col, 0), axis=0, keepdims=True)
    req_recv[pl.ds(gx, 1)] = req_send[...]

    pl.semaphore_wait(barrier, n_gx - 1 + n_gy - 1)

    def remote(src, dst, send, recv, x, y):
        return pltpu.make_async_remote_copy(
            src_ref=src,
            dst_ref=dst,
            send_sem=send,
            recv_sem=recv,
            device_id={"gx": x, "gy": y},
            device_id_type=MESH,
        )

    has_x = (gx > 0, gx < n_gx - 1)
    has_y = (gy > 0, gy < n_gy - 1)
    to_x = (jnp.maximum(gx - 1, 0), jnp.minimum(gx + 1, n_gx - 1))
    to_y = (jnp.maximum(gy - 1, 0), jnp.minimum(gy + 1, n_gy - 1))

    def first_x_copy(side, which, c, slot):
        part = pl.ds(c * CHUNK, CHUNK)
        return remote(
            (k_hbm, p_hbm)[which].at[0 if side == 0 else cx - 1, part],
            first_x.at[slot, which, part],
            fx_send.at[side, which, c],
            fx_recv.at[slot, which, c],
            to_x[side],
            gy,
        )

    def later_x_copy(turn, side, c, slot):
        return remote(
            later_x_send.at[turn - 1, side, c],
            later_x.at[turn - 1, slot, c],
            lx_send.at[turn - 1, side, c],
            lx_recv.at[turn - 1, slot, c],
            to_x[side],
            gy,
        )

    def y_copy(turn, side, slot):
        if turn == 0:
            src, dst = first_y_send.at[side], first_y.at[slot]
        else:
            src, dst = later_y_send.at[turn - 1, side], later_y.at[turn - 1, slot]
        return remote(src, dst, y_send.at[turn, side], y_recv.at[turn, slot], gx, to_y[side])

    for c in edges + middles:
        for side in range(2):

            @pl.when(has_x[side])
            def _():
                first_x_copy(side, 0, c, 1 - side).start()
                first_x_copy(side, 1, c, 1 - side).start()

    per = n_gx // n_gy
    home = gx // per
    share = gx % per

    def gather_copy():
        return remote(
            slip_send.at[0],
            slip_part.at[gy],
            gather_ssem,
            gather_rsem.at[gy],
            gx,
            home,
        )

    @pl.when(home != gy)
    def _():
        gather_copy().start()

    @pl.when(home == gy)
    def _():
        slip_part[pl.ds(gy, 1)] = slip_send[...]

    def req_copy(off):
        return remote(
            req_send.at[0],
            req_recv.at[gx],
            req_ssem.at[off],
            req_rsem.at[off],
            (gx + off) % n_gx,
            gy,
        )

    for off in range(1, n_gx):
        req_copy(off).start()

    load_k.wait()
    load_p.wait()

    def prepare(x, _):
        for j in range(nb):
            k = k_in[x, :, j * LANES : (j + 1) * LANES]
            p = p_in[x, :, j * LANES : (j + 1) * LANES]
            r = lax.rsqrt(k)
            s = k * r
            at = pl.ds(pl.multiple_of(((x + 1) * nb + j) * yp + 8, 8), cy)
            dense = pl.ds(pl.multiple_of((x * nb + j) * cy, 8), cy)
            root[at, :] = s
            u_a[at, :] = s * p
            inv[dense, :] = r
            coef_c[dense, :] = conductance * k
        return 0

    lax.fori_loop(0, cx, prepare, 0)

    n_face = cx * nb

    def face(y):
        return pl.ds(nb * yp + 8 + y, n_face, stride=yp)

    def dense_face(y):
        return pl.ds(y, n_face, stride=cy)

    y_of = (0, cy - 1)
    for side in range(2):
        first_y_send[side, 0] = root[face(y_of[side]), :]
        first_y_send[side, 1] = u_a[face(y_of[side]), :]
    for side in range(2):

        @pl.when(has_y[side])
        def _():
            y_copy(0, side, 1 - side).start()

    def around(ref, x, y0):
        here, sums = [], []
        for j in range(nb):
            at = ((x + 1) * nb + j) * yp + 8 + y0
            here.append(ref[pl.ds(pl.multiple_of(at, 8), CHUNK), :])
        for j in range(nb):
            at = ((x + 1) * nb + j) * yp + 8 + y0
            before = here[j - 1] if j > 0 else 0.0
            after = here[j + 1] if j < nb - 1 else 0.0
            left = pltpu.roll(jnp.where(lane == LANES - 1, before, here[j]), 1, 1)
            right = pltpu.roll(jnp.where(lane == 0, after, here[j]), LANES - 1, 1)
            total = ref[pl.ds(pl.multiple_of(at + nb * yp, 8), CHUNK), :]
            total = total + ref[pl.ds(pl.multiple_of(at - nb * yp, 8), CHUNK), :]
            total = total + (ref[pl.ds(at + 1, CHUNK), :] + ref[pl.ds(at - 1, CHUNK), :])
            sums.append(total + (left + right))
        return here, sums

    def sweep(turn, src, dst, inner, chunks):
        def plane(i, _):
            x = i + 2 if inner else jnp.where(i < 2, i, i + (cx - 4))
            for c in chunks:
                y0 = c * CHUNK
                here, sums = around(src, x, y0)
                if turn == 0:
                    roots, root_sums = around(root, x, y0)
                for j in range(nb):
                    dense = pl.ds(pl.multiple_of((x * nb + j) * cy + y0, 8), CHUNK)
                    if turn == 0:
                        a = 1.0 - conductance * (roots[j] * root_sums[j])
                        coef_a[dense, :] = a
                    else:
                        a = coef_a[dense, :]
                    new = a * here[j] + coef_c[dense, :] * sums[j]
                    if turn < SWEEPS - 1:
                        at = ((x + 1) * nb + j) * yp + 8 + y0
                        dst[pl.ds(pl.multiple_of(at, 8), CHUNK), :] = new
                    else:
                        out_v[x, y0 : y0 + CHUNK, j * LANES : (j + 1) * LANES] = (
                            new * inv[dense, :]
                        )
            return 0

        lax.fori_loop(0, cx - 4 if inner else 4, plane, 0)

    def fix_x(turn, side, c, src, dst):
        x = 0 if side == 0 else cx - 1
        y0 = c * CHUNK
        for j in range(nb):
            at = pl.ds(((x + 1) * nb + j) * yp + 8 + y0, CHUNK)
            dense = pl.ds((x * nb + j) * cy + y0, CHUNK)
            part = slice(j * CHUNK, (j + 1) * CHUNK)
            ys, zs = slice(y0, y0 + CHUNK), slice(j * LANES, (j + 1) * LANES)
            if turn == 0:
                k = first_x[side, 0, ys, zs]
                s = k * lax.rsqrt(k)
                halo = s * first_x[side, 1, ys, zs]
                less = conductance * (root[at, :] * s)
                coef_a[dense, :] = coef_a[dense, :] - less
                new = dst[at, :] + (coef_c[dense, :] * halo - less * src[at, :])
            else:
                halo = later_x[turn - 1, side, c, part, :]
                if turn < SWEEPS - 1:
                    new = dst[at, :] + coef_c[dense, :] * halo
            if turn < SWEEPS - 1:
                dst[at, :] = new
                later_x_send[turn, side, c, part, :] = new
            else:
                out_v[x, ys, zs] = out_v[x, ys, zs] + coef_c[dense, :] * inv[dense, :] * halo

    def take_x(turn, c, src, dst):
        for side in range(2):

            @pl.when(has_x[side])
            def _():
                if turn == 0:
                    first_x_copy(side, 0, c, side).wait_recv()
                    first_x_copy(side, 1, c, side).wait_recv()
                else:
                    later_x_copy(turn, side, c, side).wait_recv()
                fix_x(turn, side, c, src, dst)
                if turn < SWEEPS - 1:
                    later_x_copy(turn + 1, side, c, 1 - side).start()

    def take_y(turn, src, dst):
        for side in range(2):

            @pl.when(has_y[side])
            def _():
                y_copy(turn, side, side).wait_recv()
                at, dense = face(y_of[side]), dense_face(y_of[side])
                if turn == 0:
                    s, halo = first_y[side, 0], first_y[side, 1]
                    less = conductance * (root[at, :] * s)
                    coef_a[dense, :] = coef_a[dense, :] - less
                    dst[at, :] = dst[at, :] + (coef_c[dense, :] * halo - less * src[at, :])
                elif turn < SWEEPS - 1:
                    dst[at, :] = dst[at, :] + coef_c[dense, :] * later_y[turn - 1, side]
                else:
                    src[face(-1 if side == 0 else cy), :] = later_y[turn - 1, side]

    def send_y(turn, ref):
        for side in range(2):

            @pl.when(has_y[side])
            def _():
                later_y_send[turn - 1, side] = ref[face(y_of[side]), :]
                y_copy(turn, side, 1 - side).start()

    every = list(range(n_ch))
    sweep(0, u_a, u_b, True, every)
    sweep(0, u_a, u_b, False, every)

    def slip_copy(off):
        part = pl.ds(share * n_gy, n_gy)
        return remote(
            slip_part,
            slip_recv.at[part],
            slip_ssem.at[off],
            slip_rsem.at[share],
            (gx + off) % n_gx,
            gy,
        )

    @pl.when(home == gy)
    def _():
        for off in range(1, n_gy):
            other = (gy + off) % n_gy
            remote(
                slip_send.at[0], slip_part.at[other], gather_ssem, gather_rsem.at[other], gx, gy
            ).wait_recv()
        for off in range(1, n_gx):
            slip_copy(off).start()
        slip_recv[pl.ds(share * n_gy, n_gy)] = slip_part[...]

    take_y(0, u_a, u_b)
    for c in edges:
        take_x(0, c, u_a, u_b)
    send_y(1, u_b)
    sweep(1, u_b, u_a, True, every)
    for c in middles:
        take_x(0, c, u_a, u_b)
    sweep(1, u_b, u_a, False, every)

    for q in range(per):

        @pl.when(gy * per + q != gx)
        def _():
            remote(
                slip_part,
                slip_recv.at[pl.ds(q * n_gy, n_gy)],
                slip_ssem.at[0],
                slip_rsem.at[q],
                gx,
                gy,
            ).wait_recv()

    load_g.wait()
    n_cb = cols // LANES
    segment = [jnp.zeros((1, LANES), jnp.float32) for _ in range(n_cb)]
    for i in range(n_gx):
        first, shift = (i * tri) // LANES, (i * tri) % LANES
        row = slip_recv[i]
        if shift:
            row = pltpu.roll(row, shift, 1)
        segment[first] = segment[first] + jnp.where(lane >= shift, row, 0.0)
        if shift + tri > LANES:
            segment[first + 1] = segment[first + 1] + jnp.where(lane < shift, row, 0.0)
    eye_f = lax.broadcasted_iota(jnp.int32, (tri, LANES), 0) == lax.broadcasted_iota(
        jnp.int32, (tri, LANES), 1
    )
    for part in range(n_gy):
        for comp in range(2):
            total = jnp.zeros((tri, LANES), jnp.float32)
            for b in range(n_cb):
                block = g_in[comp, part * tri : (part + 1) * tri, b * LANES : (b + 1) * LANES]
                total = total + block * segment[b]
            sums = jnp.sum(total, axis=1, keepdims=True)
            part_send[part, comp : comp + 1, :] = jnp.sum(
                jnp.where(eye_f, sums, 0.0), axis=0, keepdims=True
            )

    def part_copy(off):
        to = (gy + off) % n_gy
        return remote(
            part_send.at[to], part_recv.at[gy], part_ssem.at[off], part_rsem.at[off], gx, to
        )

    part_recv[pl.ds(gy, 1)] = part_send[pl.ds(gy, 1)]
    for off in range(1, n_gy):
        part_copy(off).start()

    take_y(1, u_b, u_a)
    for c in edges:
        take_x(1, c, u_b, u_a)
    send_y(2, u_a)
    if middles:
        sweep(2, u_a, None, True, middles)

    for off in range(1, n_gx):
        remote(
            req_send.at[0],
            req_recv.at[(gx + n_gx - off) % n_gx],
            req_ssem.at[off],
            req_rsem.at[off],
            gx,
            gy,
        ).wait_recv()
    to_smem = pltpu.make_async_copy(req_recv, req_smem, load_sem.at[3])
    to_smem.start()

    for copy in loads[3:]:
        copy.wait()
    distance = vec_f[6]
    ratio = distance / vec_f[0]
    state_next = ratio + (vec_f[1] - ratio) * jnp.exp(-heal_time / ratio)
    state_ref[...] = state_next
    evolved = vec_f[5] * jnp.log(state_next / distance)

    for c in middles:
        take_x(1, c, u_b, u_a)
    take_y(2, u_a, None)
    sweep(2, u_a, None, True, edges)
    sweep(2, u_a, None, False, every)
    to_smem.wait()

    for off in range(1, n_gy):
        remote(
            part_send.at[0],
            part_recv.at[(gy + n_gy - off) % n_gy],
            part_ssem.at[off],
            part_rsem.at[off],
            gx,
            gy,
        ).wait_recv()
    rates = part_recv[0]
    for other in range(1, n_gy):
        rates = rates + part_recv[other]
    shear = vec_f[3] + step_time * rates[0:1, :tri]
    loaded = vec_f[2] + step_time * rates[1:2, :tri]

    for c in edges + middles:
        take_x(2, c, u_a, None)

    lane_z = lax.broadcasted_iota(jnp.int32, (1, nz), 1)
    if cap_pad > cap:
        ans_pick[...] = jnp.zeros_like(ans_pick)

    def answer(source, _):
        for s in range(cap):
            c = req_smem[source, 0, gx * cap + s]
            row = out_v[part_of(c, cy * nz), pl.ds(rest_of(part_of(c, nz), cy), 1), :]
            row = jnp.where(lane_z == rest_of(c, nz), row, 0.0)
            picked = row[:, :LANES]
            for j in range(1, nb):
                picked = picked + row[:, j * LANES : (j + 1) * LANES]
            ans_pick[source, s : s + 1, :] = picked
        return 0

    lax.fori_loop(0, n_gx, answer, 0)
    picks = jnp.sum(ans_pick[...], axis=2, keepdims=True)
    pick_lane = lax.broadcasted_iota(jnp.int32, (n_gx, cap_pad, width), 2)
    pick_slot = lax.broadcasted_iota(jnp.int32, (n_gx, cap_pad, width), 1)
    spread = jnp.where(
        (pick_lane == gx * cap + pick_slot) & (pick_slot < cap), picks, 0.0
    )
    ans_send[...] = jnp.sum(spread, axis=1, keepdims=True)

    def ans_copy(off):
        to = (gx + off) % n_gx
        return remote(
            ans_send.at[to], ans_recv.at[gx], ans_ssem.at[off], ans_rsem.at[off], to, gy
        )

    for off in range(1, n_gx):
        ans_copy(off).start()
    ans_recv[pl.ds(gx, 1)] = ans_send[pl.ds(gx, 1)]
    for off in range(1, n_gx):
        remote(
            ans_send.at[0],
            ans_recv.at[(gx + n_gx - off) % n_gx],
            ans_ssem.at[off],
            ans_rsem.at[off],
            gx,
            gy,
        ).wait_recv()
    answers = ans_recv[0]
    for other in range(1, n_gx):
        answers = answers + ans_recv[other]
    found = jnp.sum(jnp.where(slot_col == slot_lane, answers, 0.0), axis=1, keepdims=True)
    fault = jnp.sum(jnp.where(eye, found, 0.0), axis=0, keepdims=True)
    log_ref[...] = (shear / (loaded - fault) - friction_ref - evolved) / vec_f[4]

    for side in range(2):

        @pl.when(has_x[side])
        def _():
            for c in range(n_ch):
                first_x_copy(side, 0, c, 1 - side).wait_send()
                first_x_copy(side, 1, c, 1 - side).wait_send()
                for turn in range(1, SWEEPS):
                    later_x_copy(turn, side, c, 1 - side).wait_send()

        @pl.when(has_y[side])
        def _():
            for turn in range(SWEEPS):
                y_copy(turn, side, 1 - side).wait_send()

    @pl.when(home != gy)
    def _():
        gather_copy().wait_send()

    @pl.when(home == gy)
    def _():
        for off in range(1, n_gx):
            slip_copy(off).wait_send()

    for off in range(1, n_gx):
        req_copy(off).wait_send()
        ans_copy(off).wait_send()
    for off in range(1, n_gy):
        part_copy(off).wait_send()


def part_of(value, size):
    if size & (size - 1) == 0:
        return lax.shift_right_logical(value, jnp.int32(size.bit_length() - 1))
    return lax.div(value, jnp.int32(size))


def rest_of(value, size):
    if size & (size - 1) == 0:
        return value & (size - 1)
    return lax.rem(value, jnp.int32(size))


def write_kernel(p_ref, state_in, log_in, out_hbm, state_hbm, log_hbm, sem):
    planes = p_ref.shape[0]
    n = sem.shape[0] - 2
    writes = []
    for i in range(n):
        part = pl.ds(i * planes // n, planes // n)
        writes.append(pltpu.make_async_copy(p_ref.at[part], out_hbm.at[part], sem.at[i]))
    writes.append(pltpu.make_async_copy(state_in, state_hbm, sem.at[n]))
    writes.append(pltpu.make_async_copy(log_in, log_hbm, sem.at[n + 1]))
    for copy in writes:
        copy.start()
    for copy in writes:
        copy.wait()


def local(
    pressure,
    permeability,
    kernel,
    slip_rate,
    aging_state,
    normal_stress,
    shear_stress,
    direct_effect,
    evolution_effect,
    slip_distance,
    tri_owner,
    tri_cell,
):
    n_gx, n_gy = lax.axis_size("gx"), lax.axis_size("gy")
    cx, cy, nz = pressure.shape
    tri = slip_rate.shape[0]
    _, rows, cols = kernel.shape
    cap = max(2, 2 * tri // n_gx)
    cap_pad = -(-cap // 8) * 8
    nb = nz // LANES
    yp = cy + 8
    n_ch = cy // CHUNK
    padded = ((cx + 2) * nb * yp + 8, LANES)
    dense = (cx * nb * cy, LANES)
    width = -(-n_gx * cap // LANES) * LANES
    dims = (n_gx, n_gy, cx, cy, nz, tri, rows, cols, cap, cap_pad)
    f32, i32 = jnp.float32, jnp.int32
    dma = pltpu.SemaphoreType.DMA
    hbm = lambda a: pltpu.with_memory_space_constraint(a, pltpu.HBM)
    vec = lambda a: hbm(a.reshape(1, tri))
    any_spec = pl.BlockSpec(memory_space=pl.ANY)
    hbm_spec = pl.BlockSpec(memory_space=pltpu.HBM)
    vmem_spec = pl.BlockSpec(memory_space=pltpu.VMEM)
    out, state, log = pl.pallas_call(
        functools.partial(step_kernel, dims),
        out_shape=(
            pltpu.VMEM(pressure.shape, f32),
            pltpu.VMEM((1, tri), f32),
            pltpu.VMEM((1, tri), f32),
        ),
        in_specs=[hbm_spec] * 12,
        out_specs=(vmem_spec, vmem_spec, vmem_spec),
        scratch_shapes=[
            pltpu.VMEM(pressure.shape, f32),
            pltpu.VMEM(pressure.shape, f32),
            pltpu.VMEM(kernel.shape, f32),
            pltpu.VMEM((7, 1, tri), f32),
            pltpu.VMEM((2, 1, tri), i32),
            pltpu.VMEM(padded, f32),
            pltpu.VMEM(padded, f32),
            pltpu.VMEM(padded, f32),
            pltpu.VMEM(dense, f32),
            pltpu.VMEM(dense, f32),
            pltpu.VMEM(dense, f32),
            pltpu.VMEM((2, 2, cy, nz), f32),
            pltpu.VMEM((SWEEPS - 1, 2, n_ch, nb * CHUNK, LANES), f32),
            pltpu.VMEM((SWEEPS - 1, 2, n_ch, nb * CHUNK, LANES), f32),
            pltpu.VMEM((2, 2, cx * nb, LANES), f32),
            pltpu.VMEM((2, 2, cx * nb, LANES), f32),
            pltpu.VMEM((SWEEPS - 1, 2, cx * nb, LANES), f32),
            pltpu.VMEM((SWEEPS - 1, 2, cx * nb, LANES), f32),
            pltpu.VMEM((1, 1, LANES), f32),
            pltpu.VMEM((n_gy, 1, LANES), f32),
            pltpu.VMEM((n_gx, 1, LANES), f32),
            pltpu.VMEM((1, 1, width), i32),
            pltpu.VMEM((n_gx, 1, width), i32),
            pltpu.SMEM((n_gx, 1, width), i32),
            pltpu.VMEM((n_gy, 2, LANES), f32),
            pltpu.VMEM((n_gy, 2, LANES), f32),
            pltpu.VMEM((n_gx, cap_pad, LANES), f32),
            pltpu.VMEM((n_gx, 1, width), f32),
            pltpu.VMEM((n_gx, 1, width), f32),
            dma((4,)),
            dma((9,)),
            dma((2, 2, n_ch)),
            dma((2, 2, n_ch)),
            dma((SWEEPS - 1, 2, n_ch)),
            dma((SWEEPS - 1, 2, n_ch)),
            dma((SWEEPS, 2)),
            dma((SWEEPS, 2)),
            dma,
            dma((n_gy,)),
            dma((n_gx,)),
            dma((n_gx,)),
            dma((n_gx,)),
            dma((n_gx,)),
            dma((n_gy,)),
            dma((n_gy,)),
            dma((n_gx,)),
            dma((n_gx,)),
        ],
        compiler_params=pltpu.CompilerParams(
            collective_id=0, has_side_effects=True, vmem_limit_bytes=40 << 20
        ),
        name="fault_step",
    )(
        hbm(pressure),
        hbm(permeability),
        hbm(kernel),
        vec(slip_rate),
        vec(aging_state),
        vec(normal_stress),
        vec(shear_stress),
        vec(direct_effect),
        vec(evolution_effect),
        vec(slip_distance),
        vec(tri_owner),
        vec(tri_cell),
    )
    pieces = cx if cx < 8 else 8 if cx % 8 == 0 else 1
    out, state, log = pl.pallas_call(
        write_kernel,
        out_shape=(
            jax.ShapeDtypeStruct(pressure.shape, f32),
            jax.ShapeDtypeStruct((1, tri), f32),
            jax.ShapeDtypeStruct((1, tri), f32),
        ),
        in_specs=[vmem_spec] * 3,
        out_specs=(any_spec,) * 3,
        scratch_shapes=[dma((pieces + 2,))],
        compiler_params=pltpu.CompilerParams(vmem_limit_bytes=4 << 20),
        name="write_out",
    )(out, state, log)
    return out, state.reshape(tri), log.reshape(tri)


def solution(mesh):
    fault = P(("gx", "gy"))
    field = P("gx", "gy", None)
    in_specs = (field, field, P(None, "gx", "gy")) + (fault,) * 7 + (P(("gx", "gy"), None), fault)
    out_specs = (field, fault, fault)
    return jax.shard_map(local, mesh=mesh, in_specs=in_specs, out_specs=out_specs, check_vma=False)
```

```python
import functools

import jax
import jax.numpy as jnp
from jax import lax
from jax.experimental import pallas as pl
from jax.experimental.pallas import tpu as pltpu
from jax.sharding import PartitionSpec as P

SWEEPS = 3
LANES = 128
CHUNK = 16
MESH = pl.DeviceIdType.MESH

conductance = 0.15
step_time = 1.0
heal_time = 0.5
friction_ref = 0.6


def step_kernel(
    dims,
    p_hbm,
    k_hbm,
    g_hbm,
    slip_hbm,
    aging_hbm,
    normal_hbm,
    shear_hbm,
    direct_hbm,
    evolution_hbm,
    distance_hbm,
    owner_hbm,
    cell_hbm,
    out_v,
    state_ref,
    log_ref,
    p_in,
    k_in,
    g_in,
    vec_f,
    vec_i,
    root,
    u_a,
    u_b,
    coef_a,
    coef_c,
    inv,
    first_x,
    relay_x,
    later_x_send,
    later_x,
    first_y_send,
    first_y,
    later_y_send,
    later_y,
    corner_send,
    corner,
    slip_send,
    slip_part,
    slip_recv,
    req_send,
    req_recv,
    req_at,
    req_smem,
    part_send,
    part_recv,
    pick_a,
    pick_b,
    pick_n,
    pick_c,
    ans_send,
    ans_recv,
    load_sem,
    vec_sem,
    x_send,
    fx_recv,
    lx_recv,
    relay_send,
    relay_recv,
    y_send,
    y_recv,
    corner_recv,
    row_sem,
    col_sem,
    gather_ssem,
    gather_rsem,
    slip_ssem,
    slip_rsem,
    req_ssem,
    req_rsem,
    part_ssem,
    part_rsem,
    ans_ssem,
    ans_rsem,
):
    n_gx, n_gy, cx, cy, nz, tri, rows, cols, cap, cap_pad = dims
    nb = nz // LANES
    yp = cy + 8
    n_ch = cy // CHUNK
    edges = sorted({0, n_ch - 1})
    middles = [c for c in range(n_ch) if c not in edges]
    gx, gy = lax.axis_index("gx"), lax.axis_index("gy")
    lane = lax.broadcasted_iota(jnp.int32, (1, LANES), 1)

    early = (
        (owner_hbm, vec_i.at[0], vec_sem.at[0]),
        (cell_hbm, vec_i.at[1], vec_sem.at[0]),
        (slip_hbm, vec_f.at[0], vec_sem.at[1]),
    )
    late = (aging_hbm, normal_hbm, shear_hbm, direct_hbm, evolution_hbm, distance_hbm)
    half = cx // 2

    def load(which, part):
        src, dst = ((k_hbm, k_in), (p_hbm, p_in))[which]
        at = pl.ds(part * half, half)
        return pltpu.make_async_copy(src.at[at], dst.at[at], load_sem.at[which, part])

    load_g = pltpu.make_async_copy(g_hbm, g_in, vec_sem.at[3])

    barrier = pltpu.get_barrier_semaphore()

    def greet(x, y):
        pl.semaphore_signal(barrier, inc=1, device_id={"gx": x, "gy": y}, device_id_type=MESH)

    has_x = (gx > 0, gx < n_gx - 1)
    has_y = (gy > 0, gy < n_gy - 1)
    to_x = (jnp.maximum(gx - 1, 0), jnp.minimum(gx + 1, n_gx - 1))
    to_y = (jnp.maximum(gy - 1, 0), jnp.minimum(gy + 1, n_gy - 1))
    mid = n_gx // 2
    relayed = middles[:2] if n_gx >= 8 and len(middles) >= 2 else []
    is_mid = (gx == mid, gx == mid - 1)
    is_end = (gx == 0, gx == n_gx - 1)
    if relayed:
        on_relay = is_mid[0] | is_mid[1] | is_end[0] | is_end[1]
        partners = (
            jnp.where(is_end[0] | is_end[1], mid, 0),
            jnp.where(is_end[0] | is_end[1], mid - 1, n_gx - 1),
        )

    greeted = jnp.int32(0)
    for side in range(2):

        @pl.when(has_x[side])
        def _():
            greet(to_x[side], gy)

        @pl.when(has_y[side])
        def _():
            greet(gx, to_y[side])

        greeted = greeted + jnp.where(has_x[side], 1, 0) + jnp.where(has_y[side], 1, 0)
    if relayed:

        @pl.when(on_relay)
        def _():
            for partner in partners:
                greet(partner, gy)

        greeted = greeted + jnp.where(on_relay, 2, 0)

    for src, dst, sem in early:
        pltpu.make_async_copy(src, dst, sem).start()
    for part in range(2):
        for which in range(2):
            load(which, part).start()

    zero = jnp.zeros((8, LANES), jnp.float32)
    n_col = (cx + 2) * nb
    for ref in (root, u_a, u_b):
        for c in range(nb, n_col - nb + 1):
            ref[c * yp : c * yp + 8, :] = zero
        ref[0 : nb * yp, :] = jnp.zeros((nb * yp, LANES), jnp.float32)
        ref[(cx + 1) * nb * yp : (cx + 2) * nb * yp + 8, :] = jnp.zeros(
            (nb * yp + 8, LANES), jnp.float32
        )

    for ref in (pick_a, pick_b, pick_n, pick_c):
        ref[...] = jnp.zeros_like(ref)
    pl.semaphore_wait(barrier, greeted)

    def remote(src, dst, send, recv, x, y):
        return pltpu.make_async_remote_copy(
            src_ref=src,
            dst_ref=dst,
            send_sem=send,
            recv_sem=recv,
            device_id={"gx": x, "gy": y},
            device_id_type=MESH,
        )

    def first_x_copy(side, which, c):
        part = pl.ds(c * CHUNK, CHUNK)
        return remote(
            (k_hbm, p_hbm)[which].at[0 if side == 0 else cx - 1, part],
            first_x.at[1 - side, which, part],
            x_send.at[side],
            fx_recv.at[1 - side, c],
            to_x[side],
            gy,
        )

    def to_relay(side, which, i):
        part = pl.ds(relayed[i] * CHUNK, CHUNK)
        return remote(
            (k_hbm, p_hbm)[which].at[0 if side == 0 else cx - 1, part],
            relay_x.at[i, which],
            x_send.at[side],
            relay_recv.at[i],
            0 if side == 0 else n_gx - 1,
            gy,
        )

    def from_relay(side, i):
        return remote(
            relay_x.at[i],
            first_x.at[1 - side, :, pl.ds(relayed[i] * CHUNK, CHUNK)],
            relay_send,
            fx_recv.at[1 - side, relayed[i]],
            mid - 1 if side == 0 else mid,
            gy,
        )

    def pass_on(i):
        for side in range(2):

            @pl.when(is_end[side])
            def _():
                pltpu.make_async_copy(relay_x.at[i], relay_x.at[i], relay_recv.at[i]).wait()
                from_relay(side, i).start()

    def later_x_copy(turn, side, c):
        return remote(
            later_x_send.at[turn - 1, side, c],
            later_x.at[turn - 1, 1 - side, c],
            x_send.at[side],
            lx_recv.at[turn - 1, 1 - side, c],
            to_x[side],
            gy,
        )

    def landed(ref, sem):
        pltpu.make_async_copy(ref, ref, sem).wait()

    def y_copy(turn, side):
        if turn == 0:
            src, dst = first_y_send.at[side], first_y.at[1 - side]
        else:
            src, dst = later_y_send.at[turn - 1, side], later_y.at[turn - 1, 1 - side]
        return remote(src, dst, y_send.at[side], y_recv.at[turn, 1 - side], gx, to_y[side])

    def corner_copy(turn, side):
        return remote(
            corner_send.at[turn - 1, side],
            corner.at[turn - 1, 1 - side],
            y_send.at[side],
            corner_recv.at[turn - 1, 1 - side],
            gx,
            to_y[side],
        )

    for c in edges + middles:
        for side in range(2):
            direct = has_x[side]
            if c in relayed:
                direct = direct & jnp.logical_not(is_mid[side])

                @pl.when(is_mid[side])
                def _():
                    to_relay(side, 0, relayed.index(c)).start()
                    to_relay(side, 1, relayed.index(c)).start()

            @pl.when(direct)
            def _():
                first_x_copy(side, 0, c).start()
                first_x_copy(side, 1, c).start()

    rounds = [], []
    for axis, size in enumerate((n_gx, n_gy)):
        reach = 1
        while reach < size - 1:
            rounds[axis].append(reach)
            reach *= 2
    n_rounds = max(len(r) for r in rounds)

    def round_peers(k):
        for axis, (me, size, sem) in enumerate(((gx, n_gx, row_sem), (gy, n_gy, col_sem))):
            if k < len(rounds[axis]):
                d = rounds[axis][k]
                low, high = jnp.maximum(me - d, 0), jnp.minimum(me + d, size - 1)
                to = [(i, gy) if axis == 0 else (gx, i) for i in (low, high)]
                yield (me >= d, me + d < size), to, sem.at[k]

    def tell(k):
        for has, to, sem in round_peers(k):
            for side in range(2):

                @pl.when(has[side])
                def _():
                    pl.semaphore_signal(
                        sem,
                        inc=1,
                        device_id={"gx": to[side][0], "gy": to[side][1]},
                        device_id_type=MESH,
                    )

    def hear(k):
        for has, _, sem in round_peers(k):
            pl.semaphore_wait(sem, jnp.where(has[0], 1, 0) + jnp.where(has[1], 1, 0))

    tell(0)

    pltpu.make_async_copy(vec_i, vec_i, vec_sem.at[0]).wait()
    pltpu.make_async_copy(vec_f.at[0], vec_f.at[0], vec_sem.at[1]).wait()
    slip_send[...] = jnp.zeros_like(slip_send)
    slip_send[0, :, :tri] = vec_f[0]

    owner_row = vec_i[0]
    cell_row = vec_i[1]
    t_row = lax.broadcasted_iota(jnp.int32, (tri, tri), 1)
    t_col = lax.broadcasted_iota(jnp.int32, (tri, tri), 0)
    eye = t_row == t_col
    owner_wide = jnp.broadcast_to(owner_row, (tri, tri))
    owner_col = jnp.sum(jnp.where(eye, owner_wide, 0), axis=1, keepdims=True)
    cell_col = jnp.sum(
        jnp.where(eye, jnp.broadcast_to(cell_row, (tri, tri)), 0), axis=1, keepdims=True
    )
    same = owner_col == owner_wide
    one_below = jnp.where(same & (t_row < t_col), 1, 0)
    rank_col = jnp.sum(one_below, axis=1, keepdims=True)
    slot_col = owner_col * cap + rank_col
    width = req_send.shape[-1]
    slot_lane = lax.broadcasted_iota(jnp.int32, (tri, width), 1)
    req_send[0] = jnp.sum(jnp.where(slot_col == slot_lane, cell_col, 0), axis=0, keepdims=True)
    req_recv[pl.ds(gx, 1)] = req_send[...]

    def prepare(x, _):
        for j in range(nb):
            k = k_in[x, :, j * LANES : (j + 1) * LANES]
            p = p_in[x, :, j * LANES : (j + 1) * LANES]
            r = lax.rsqrt(k)
            s = k * r
            at = pl.ds(pl.multiple_of(((x + 1) * nb + j) * yp + 8, 8), cy)
            dense = pl.ds(pl.multiple_of((x * nb + j) * cy, 8), cy)
            root[at, :] = s
            u_a[at, :] = s * p
            inv[dense, :] = r
            coef_c[dense, :] = conductance * k
        return 0

    for part in range(2):
        load(0, part).wait()
        load(1, part).wait()
        lax.fori_loop(part * half, (part + 1) * half, prepare, 0)
    load_g.start()
    for i, src in enumerate(late):
        pltpu.make_async_copy(src, vec_f.at[1 + i], vec_sem.at[2]).start()

    n_face = cx * nb

    def face(y):
        return pl.ds(nb * yp + 8 + y, n_face, stride=yp)

    def dense_face(y):
        return pl.ds(y, n_face, stride=cy)

    y_of = (0, cy - 1)
    for side in range(2):
        first_y_send[side, 0] = root[face(y_of[side]), :]
        first_y_send[side, 1] = u_a[face(y_of[side]), :]
    for side in range(2):

        @pl.when(has_y[side])
        def _():
            y_copy(0, side).start()

    def around(ref, x, y0):
        here, sums = [], []
        for j in range(nb):
            at = ((x + 1) * nb + j) * yp + 8 + y0
            here.append(ref[at : at + CHUNK, :])
        for j in range(nb):
            at = ((x + 1) * nb + j) * yp + 8 + y0
            before = here[j - 1] if j > 0 else 0.0
            after = here[j + 1] if j < nb - 1 else 0.0
            left = pltpu.roll(jnp.where(lane == LANES - 1, before, here[j]), 1, 1)
            right = pltpu.roll(jnp.where(lane == 0, after, here[j]), LANES - 1, 1)
            step = nb * yp
            total = ref[at + step : at + step + CHUNK, :] + ref[at - step : at - step + CHUNK, :]
            total = total + (ref[at + 1 : at + 1 + CHUNK, :] + ref[at - 1 : at - 1 + CHUNK, :])
            sums.append(total + (left + right))
        return here, sums

    def sweep(turn, src, dst, planes, chunks):
        for x in planes:
            for c in chunks:
                y0 = c * CHUNK
                here, sums = around(src, x, y0)
                if turn == 0:
                    roots, root_sums = around(root, x, y0)
                for j in range(nb):
                    at = ((x + 1) * nb + j) * yp + 8 + y0
                    dense = (x * nb + j) * cy + y0
                    if turn == 0:
                        a = 1.0 - conductance * (roots[j] * root_sums[j])
                        coef_a[dense : dense + CHUNK, :] = a
                    else:
                        a = coef_a[dense : dense + CHUNK, :]
                    new = a * here[j] + coef_c[dense : dense + CHUNK, :] * sums[j]
                    if turn < SWEEPS - 1:
                        dst[at : at + CHUNK, :] = new
                    else:
                        out_v[x, y0 : y0 + CHUNK, j * LANES : (j + 1) * LANES] = (
                            new * inv[dense : dense + CHUNK, :]
                        )

    def fix_x(turn, side, c, src, dst):
        x = 0 if side == 0 else cx - 1
        y0 = c * CHUNK
        for j in range(nb):
            at = pl.ds(((x + 1) * nb + j) * yp + 8 + y0, CHUNK)
            dense = pl.ds((x * nb + j) * cy + y0, CHUNK)
            part = slice(j * CHUNK, (j + 1) * CHUNK)
            ys, zs = slice(y0, y0 + CHUNK), slice(j * LANES, (j + 1) * LANES)
            if turn == 0:
                k = first_x[side, 0, ys, zs]
                s = k * lax.rsqrt(k)
                halo = s * first_x[side, 1, ys, zs]
                less = conductance * (root[at, :] * s)
                coef_a[dense, :] = coef_a[dense, :] - less
                new = dst[at, :] + (coef_c[dense, :] * halo - less * src[at, :])
            else:
                halo = later_x[turn - 1, side, c, part, :]
                if turn < SWEEPS - 1:
                    new = dst[at, :] + coef_c[dense, :] * halo
            if turn < SWEEPS - 1:
                dst[at, :] = new
                later_x_send[turn, side, c, part, :] = new
            else:
                out_v[x, ys, zs] = out_v[x, ys, zs] + coef_c[dense, :] * inv[dense, :] * halo

    def take_x(turn, c, src, dst):
        for side in range(2):

            @pl.when(has_x[side])
            def _():
                if turn == 0:
                    landed(first_x.at[side, :, pl.ds(c * CHUNK, CHUNK)], fx_recv.at[side, c])
                else:
                    landed(later_x.at[turn - 1, side, c], lx_recv.at[turn - 1, side, c])
                fix_x(turn, side, c, src, dst)
                if turn < SWEEPS - 1:
                    later_x_copy(turn + 1, side, c).start()

    n_inner = (cx - 2) * nb

    def inner_face(y):
        return pl.ds(2 * nb * yp + 8 + y, n_inner, stride=yp)

    def inner_dense(y):
        return pl.ds(nb * cy + y, n_inner, stride=cy)

    def corner_faces(y):
        for i, x in enumerate((0, cx - 1)):
            yield (
                pl.ds((x + 1) * nb * yp + 8 + y, nb, stride=yp),
                pl.ds(x * nb * cy + y, nb, stride=cy),
                slice(i * nb, (i + 1) * nb),
            )

    def take_y(turn, src, dst):
        for side in range(2):

            @pl.when(has_y[side])
            def _():
                if turn == 0:
                    landed(first_y.at[side], y_recv.at[turn, side])
                    at, dense = face(y_of[side]), dense_face(y_of[side])
                    s, halo = first_y[side, 0], first_y[side, 1]
                    less = conductance * (root[at, :] * s)
                    coef_a[dense, :] = coef_a[dense, :] - less
                    dst[at, :] = dst[at, :] + (coef_c[dense, :] * halo - less * src[at, :])
                else:
                    landed(later_y.at[turn - 1, side], y_recv.at[turn, side])
                    if turn < SWEEPS - 1:
                        at, dense = inner_face(y_of[side]), inner_dense(y_of[side])
                        dst[at, :] = dst[at, :] + coef_c[dense, :] * later_y[turn - 1, side]
                    else:
                        src[inner_face(-1 if side == 0 else cy), :] = later_y[turn - 1, side]

    def take_corner(turn, src, dst):
        for side in range(2):

            @pl.when(has_y[side])
            def _():
                landed(corner.at[turn - 1, side], corner_recv.at[turn - 1, side])
                if turn < SWEEPS - 1:
                    for at, dense, part in corner_faces(y_of[side]):
                        dst[at, :] = dst[at, :] + coef_c[dense, :] * corner[turn - 1, side, part, :]
                else:
                    for at, _, part in corner_faces(-1 if side == 0 else cy):
                        src[at, :] = corner[turn - 1, side, part, :]

    def send_y(turn, ref):
        for side in range(2):

            @pl.when(has_y[side])
            def _():
                later_y_send[turn - 1, side] = ref[inner_face(y_of[side]), :]
                y_copy(turn, side).start()

    def send_corner(turn, ref):
        for side in range(2):

            @pl.when(has_y[side])
            def _():
                for at, _, part in corner_faces(y_of[side]):
                    corner_send[turn - 1, side, part, :] = ref[at, :]
                corner_copy(turn, side).start()

    every = list(range(n_ch))
    inner, outer = range(2, cx - 2), (0, 1, cx - 2, cx - 1)
    per = n_gx // n_gy
    home = gx // per
    share = gx % per

    def gather_copy():
        return remote(slip_send.at[0], slip_part.at[gy], gather_ssem, gather_rsem, gx, home)

    def gather_slip():
        @pl.when(home != gy)
        def _():
            gather_copy().start()

        @pl.when(home == gy)
        def _():
            slip_part[pl.ds(gy, 1)] = slip_send[...]

    def round_done(k):
        hear(k)
        if k == len(rounds[1]) - 1:
            gather_slip()

    round_done(0)
    tell(1)
    sweep(0, u_a, u_b, range(half), every)
    if relayed:
        pass_on(0)
    round_done(1)
    tell(2)
    sweep(0, u_a, u_b, range(half, cx), every)
    if relayed:
        pass_on(1)
    round_done(2)
    for k in range(3, n_rounds):
        tell(k)
        round_done(k)

    def req_copy(off):
        return remote(
            req_send.at[0], req_recv.at[gx], req_ssem, req_rsem, (gx + off) % n_gx, gy
        )

    for off in range(1, n_gx):
        req_copy(off).start()

    def slip_copy(off):
        part = pl.ds(share * n_gy, n_gy)
        return remote(
            slip_part.at[pl.ds(0, n_gy)], slip_recv.at[part], slip_ssem, slip_rsem, (gx + off) % n_gx, gy
        )

    def spread_slip():
        @pl.when(home == gy)
        def _():
            landed(slip_part.at[pl.ds(0, n_gy - 1)], gather_rsem)
            for off in range(1, n_gx):
                slip_copy(off).start()
            slip_recv[pl.ds(share * n_gy, n_gy)] = slip_part[:n_gy]

    take_y(0, u_a, u_b)
    send_y(1, u_b)
    for c in edges:
        take_x(0, c, u_a, u_b)
    send_corner(1, u_b)
    sweep(1, u_b, u_a, inner, every)
    for c in middles:
        take_x(0, c, u_a, u_b)
    spread_slip()
    sweep(1, u_b, u_a, outer, every)

    take_y(1, u_b, u_a)
    send_y(2, u_a)
    take_corner(1, u_b, u_a)
    for c in edges:
        take_x(1, c, u_b, u_a)
    send_corner(2, u_a)
    if middles:
        sweep(2, u_a, None, inner, middles)

    landed(req_recv.at[pl.ds(0, n_gx - 1)], req_rsem)
    asked = req_recv[...]
    at_x, in_x = part_of(asked, cy * nz), rest_of(asked, cy * nz)
    at_y, at_z = part_of(in_x, nz), rest_of(in_x, nz)
    at_j, at_l = part_of(at_z, LANES), rest_of(at_z, LANES)
    owner_lane = lax.broadcasted_iota(jnp.int32, asked.shape, 2)
    above, below = owner_lane >= (gx + 1) * cap, owner_lane < gx * cap
    req_at[0] = ((at_x + 1) * nb + at_j) * yp + 8 + at_y
    req_at[1] = (at_x * nb + at_j) * cy + at_y
    req_at[2] = at_l
    req_at[3] = jnp.where(at_z == 0, -1, at_l + (LANES - 1))
    req_at[4] = jnp.where(at_z == nz - 1, -1, at_l - (LANES - 1))
    req_at[5] = (jnp.where(above, cx, 1) * nb + at_j) * yp + 8 + at_y
    req_at[6] = jnp.where((above & (at_x == 0)) | (below & (at_x == cx - 1)), at_l, -1)
    to_smem = pltpu.make_async_copy(req_at, req_smem, vec_sem.at[0])
    to_smem.start()

    landed(vec_f.at[pl.ds(1, len(late))], vec_sem.at[2])
    distance = vec_f[6]
    ratio = distance / vec_f[0]
    state_next = ratio + (vec_f[1] - ratio) * jnp.exp(-heal_time / ratio)
    state_ref[...] = state_next
    evolved = vec_f[5] * jnp.log(state_next / distance)

    for c in middles:
        take_x(1, c, u_b, u_a)
    to_smem.wait()

    def across(source, _):
        for s in range(2 * cap):
            if s < cap:
                slot = jnp.minimum((gx + 1) * cap + s, width - 1)
            else:
                slot = jnp.maximum((gx - 2) * cap + s, 0)
            row = u_a[pl.ds(req_smem[5, source, 0, slot], 1), :]
            pick_c[source, s : s + 1, :] = jnp.where(
                lane == req_smem[6, source, 0, slot], row, 0.0
            )
        return 0

    lax.fori_loop(0, n_gx, across, 0)
    take_y(2, u_a, None)
    take_corner(2, u_a, None)

    def answer(source, _):
        for s in range(cap):
            slot = gx * cap + s
            at = req_smem[0, source, 0, slot]
            dense = pl.ds(req_smem[1, source, 0, slot], 1)
            z = req_smem[2, source, 0, slot]
            here = u_a[pl.ds(at, 1), :]
            step = nb * yp
            beside = (u_a[pl.ds(at + step, 1), :] + u_a[pl.ds(at - step, 1), :]) + (
                u_a[pl.ds(at + 1, 1), :] + u_a[pl.ds(at - 1, 1), :]
            )
            near = jnp.where((lane == z - 1) | (lane == z + 1), here, 0.0)
            near = near + jnp.where(
                lane == req_smem[3, source, 0, slot], u_a[pl.ds(at - yp, 1), :], 0.0
            )
            near = near + jnp.where(
                lane == req_smem[4, source, 0, slot], u_a[pl.ds(at + yp, 1), :], 0.0
            )
            back = inv[dense, :]
            weight = coef_c[dense, :] * back
            pick_a[source, s : s + 1, :] = jnp.where(
                lane == z, (coef_a[dense, :] * here) * back + weight * beside, 0.0
            )
            pick_b[source, s : s + 1, :] = jnp.where(lane == z, weight, 0.0)
            pick_n[source, s : s + 1, :] = near
        return 0

    lax.fori_loop(0, n_gx, answer, 0)

    def spread(values, first):
        n = values.shape[1]
        to_lane = lax.broadcasted_iota(jnp.int32, (n_gx, n, width), 2)
        of_slot = lax.broadcasted_iota(jnp.int32, (n_gx, n, width), 1)
        return jnp.sum(jnp.where(to_lane == first(of_slot), values, 0.0), axis=1, keepdims=True)

    def own(slot):
        return jnp.where(slot < cap, gx * cap + slot, -1)

    def beyond(slot):
        upper = jnp.where(slot < cap, (gx + 1) * cap + slot, (gx - 2) * cap + slot)
        return jnp.where(slot < 2 * cap, upper, -1)

    weights = jnp.sum(pick_b[...], axis=2, keepdims=True)
    values = jnp.sum(pick_a[...], axis=2, keepdims=True) + weights * jnp.sum(
        pick_n[...], axis=2, keepdims=True
    )
    ans_send[:, 0] = spread(values, own)
    ans_send[:, 1] = spread(weights, own)
    ans_send[:, 2] = spread(jnp.sum(pick_c[...], axis=2, keepdims=True), beyond)

    def ans_copy(off):
        to = (gx + off) % n_gx
        return remote(
            ans_send.at[to], ans_recv.at[gx], ans_ssem, ans_rsem, to, gy
        )

    for off in range(1, n_gx):
        ans_copy(off).start()
    ans_recv[pl.ds(gx, 1)] = ans_send[pl.ds(gx, 1)]

    @pl.when(home != gy)
    def _():
        landed(slip_recv.at[pl.ds(0, per * n_gy)], slip_rsem)

    if per > 1:

        @pl.when(home == gy)
        def _():
            landed(slip_recv.at[pl.ds(0, (per - 1) * n_gy)], slip_rsem)

    load_g.wait()
    n_cb = cols // LANES
    segment = [jnp.zeros((1, LANES), jnp.float32) for _ in range(n_cb)]
    for i in range(n_gx):
        first, shift = (i * tri) // LANES, (i * tri) % LANES
        row = slip_recv[i]
        if shift:
            row = pltpu.roll(row, shift, 1)
        segment[first] = segment[first] + jnp.where(lane >= shift, row, 0.0)
        if shift + tri > LANES:
            segment[first + 1] = segment[first + 1] + jnp.where(lane < shift, row, 0.0)
    eye_f = lax.broadcasted_iota(jnp.int32, (tri, LANES), 0) == lax.broadcasted_iota(
        jnp.int32, (tri, LANES), 1
    )
    for part in range(n_gy):
        for comp in range(2):
            total = jnp.zeros((tri, LANES), jnp.float32)
            for b in range(n_cb):
                block = g_in[comp, part * tri : (part + 1) * tri, b * LANES : (b + 1) * LANES]
                total = total + block * segment[b]
            sums = jnp.sum(total, axis=1, keepdims=True)
            part_send[part, comp : comp + 1, :] = jnp.sum(
                jnp.where(eye_f, sums, 0.0), axis=0, keepdims=True
            )

    def part_copy(off):
        to = (gy + off) % n_gy
        return remote(
            part_send.at[to], part_recv.at[gy], part_ssem, part_rsem, gx, to
        )

    part_recv[pl.ds(gy, 1)] = part_send[pl.ds(gy, 1)]
    for off in range(1, n_gy):
        part_copy(off).start()


    sweep(2, u_a, None, inner, edges)
    sweep(2, u_a, None, outer, every)
    for c in edges + middles:
        take_x(2, c, u_a, None)

    landed(ans_recv.at[pl.ds(0, n_gx - 1)], ans_rsem)
    answers = [ans_recv[0, i] for i in range(3)]
    for other in range(1, n_gx):
        answers = [answers[i] + ans_recv[other, i] for i in range(3)]
    answers = answers[0] + answers[1] * answers[2]
    found = jnp.sum(jnp.where(slot_col == slot_lane, answers, 0.0), axis=1, keepdims=True)
    fault = jnp.sum(jnp.where(eye, found, 0.0), axis=0, keepdims=True)
    landed(part_recv.at[pl.ds(0, n_gy - 1)], part_rsem)
    rates = part_recv[0]
    for other in range(1, n_gy):
        rates = rates + part_recv[other]
    shear = vec_f[3] + step_time * rates[0:1, :tri]
    loaded = vec_f[2] + step_time * rates[1:2, :tri]
    log_ref[...] = (shear / (loaded - fault) - friction_ref - evolved) / vec_f[4]

    for side in range(2):

        @pl.when(has_x[side])
        def _():
            landed(p_in.at[pl.ds(0, SWEEPS + 1)], x_send.at[side])

        @pl.when(has_y[side])
        def _():
            landed(coef_a.at[pl.ds(0, (SWEEPS + 1) * n_face)], y_send.at[side])

        if relayed:

            @pl.when(is_end[side])
            def _():
                landed(relay_x, relay_send)

    @pl.when(home != gy)
    def _():
        gather_copy().wait_send()

    @pl.when(home == gy)
    def _():
        landed(slip_part, slip_ssem)

    landed(req_recv.at[pl.ds(0, n_gx - 1)], req_ssem)
    landed(ans_recv.at[pl.ds(0, n_gx - 1)], ans_ssem)
    landed(part_recv.at[pl.ds(0, n_gy - 1)], part_ssem)


def part_of(value, size):
    if size & (size - 1) == 0:
        return lax.shift_right_logical(value, jnp.int32(size.bit_length() - 1))
    return lax.div(value, jnp.int32(size))


def rest_of(value, size):
    if size & (size - 1) == 0:
        return value & (size - 1)
    return lax.rem(value, jnp.int32(size))


def write_kernel(p_ref, state_in, log_in, out_hbm, state_hbm, log_hbm, sem):
    planes = p_ref.shape[0]
    n = 4 if planes % 4 == 0 else 1
    for i in range(n):
        part = pl.ds(i * planes // n, planes // n)
        pltpu.make_async_copy(p_ref.at[part], out_hbm.at[part], sem.at[0]).start()
    small = [
        pltpu.make_async_copy(state_in, state_hbm, sem.at[1]),
        pltpu.make_async_copy(log_in, log_hbm, sem.at[2]),
    ]
    for copy in small:
        copy.start()
    pltpu.make_async_copy(p_ref, out_hbm, sem.at[0]).wait()
    for copy in small:
        copy.wait()


def local(
    pressure,
    permeability,
    kernel,
    slip_rate,
    aging_state,
    normal_stress,
    shear_stress,
    direct_effect,
    evolution_effect,
    slip_distance,
    tri_owner,
    tri_cell,
):
    n_gx, n_gy = lax.axis_size("gx"), lax.axis_size("gy")
    cx, cy, nz = pressure.shape
    tri = slip_rate.shape[0]
    _, rows, cols = kernel.shape
    cap = max(2, 2 * tri // n_gx)
    cap_pad = -(-cap // 8) * 8
    nb = nz // LANES
    yp = cy + 8
    n_ch = cy // CHUNK
    padded = ((cx + 2) * nb * yp + 8, LANES)
    dense = (cx * nb * cy, LANES)
    width = -(-n_gx * cap // LANES) * LANES
    dims = (n_gx, n_gy, cx, cy, nz, tri, rows, cols, cap, cap_pad)
    f32, i32 = jnp.float32, jnp.int32
    dma = pltpu.SemaphoreType.DMA
    hbm = lambda a: pltpu.with_memory_space_constraint(a, pltpu.HBM)
    vec = lambda a: hbm(a.reshape(1, tri))
    any_spec = pl.BlockSpec(memory_space=pl.ANY)
    hbm_spec = pl.BlockSpec(memory_space=pltpu.HBM)
    vmem_spec = pl.BlockSpec(memory_space=pltpu.VMEM)
    out, state, log = pl.pallas_call(
        functools.partial(step_kernel, dims),
        out_shape=(
            pltpu.VMEM(pressure.shape, f32),
            pltpu.VMEM((1, tri), f32),
            pltpu.VMEM((1, tri), f32),
        ),
        in_specs=[hbm_spec] * 12,
        out_specs=(vmem_spec, vmem_spec, vmem_spec),
        scratch_shapes=[
            pltpu.VMEM(pressure.shape, f32),
            pltpu.VMEM(pressure.shape, f32),
            pltpu.VMEM(kernel.shape, f32),
            pltpu.VMEM((7, 1, tri), f32),
            pltpu.VMEM((2, 1, tri), i32),
            pltpu.VMEM(padded, f32),
            pltpu.VMEM(padded, f32),
            pltpu.VMEM(padded, f32),
            pltpu.VMEM(dense, f32),
            pltpu.VMEM(dense, f32),
            pltpu.VMEM(dense, f32),
            pltpu.VMEM((2, 2, cy, nz), f32),
            pltpu.VMEM((2, 2, CHUNK, nz), f32),
            pltpu.VMEM((SWEEPS - 1, 2, n_ch, nb * CHUNK, LANES), f32),
            pltpu.VMEM((SWEEPS - 1, 2, n_ch, nb * CHUNK, LANES), f32),
            pltpu.VMEM((2, 2, cx * nb, LANES), f32),
            pltpu.VMEM((2, 2, cx * nb, LANES), f32),
            pltpu.VMEM((SWEEPS - 1, 2, (cx - 2) * nb, LANES), f32),
            pltpu.VMEM((SWEEPS - 1, 2, (cx - 2) * nb, LANES), f32),
            pltpu.VMEM((SWEEPS - 1, 2, 2 * nb, LANES), f32),
            pltpu.VMEM((SWEEPS - 1, 2, 2 * nb, LANES), f32),
            pltpu.VMEM((1, 1, LANES), f32),
            pltpu.VMEM((n_gy * (n_gx - 1), 1, LANES), f32),
            pltpu.VMEM((n_gx, 1, LANES), f32),
            pltpu.VMEM((1, 1, width), i32),
            pltpu.VMEM((n_gx, 1, width), i32),
            pltpu.VMEM((7, n_gx, 1, width), i32),
            pltpu.SMEM((7, n_gx, 1, width), i32),
            pltpu.VMEM((n_gy, 2, LANES), f32),
            pltpu.VMEM((n_gy, 2, LANES), f32),
            pltpu.VMEM((n_gx, cap_pad, LANES), f32),
            pltpu.VMEM((n_gx, cap_pad, LANES), f32),
            pltpu.VMEM((n_gx, cap_pad, LANES), f32),
            pltpu.VMEM((n_gx, -(-2 * cap // 8) * 8, LANES), f32),
            pltpu.VMEM((n_gx, 3, 1, width), f32),
            pltpu.VMEM((n_gx, 3, 1, width), f32),
            dma((2, 2)),
            dma((4,)),
            dma((2,)),
            dma((2, n_ch)),
            dma((SWEEPS - 1, 2, n_ch)),
            dma,
            dma((2,)),
            dma((2,)),
            dma((SWEEPS, 2)),
            dma((SWEEPS - 1, 2)),
            pltpu.SemaphoreType.REGULAR((max(1, (n_gx - 2).bit_length()),)),
            pltpu.SemaphoreType.REGULAR((max(1, (n_gy - 2).bit_length()),)),
            dma,
            dma,
            dma,
            dma,
            dma,
            dma,
            dma,
            dma,
            dma,
            dma,
        ],
        compiler_params=pltpu.CompilerParams(
            collective_id=0, has_side_effects=True, vmem_limit_bytes=40 << 20
        ),
        name="fault_step",
    )(
        hbm(pressure),
        hbm(permeability),
        hbm(kernel),
        vec(slip_rate),
        vec(aging_state),
        vec(normal_stress),
        vec(shear_stress),
        vec(direct_effect),
        vec(evolution_effect),
        vec(slip_distance),
        vec(tri_owner),
        vec(tri_cell),
    )
    out, state, log = pl.pallas_call(
        write_kernel,
        out_shape=(
            jax.ShapeDtypeStruct(pressure.shape, f32),
            jax.ShapeDtypeStruct((1, tri), f32),
            jax.ShapeDtypeStruct((1, tri), f32),
        ),
        in_specs=[vmem_spec] * 3,
        out_specs=(any_spec,) * 3,
        scratch_shapes=[dma((3,))],
        compiler_params=pltpu.CompilerParams(vmem_limit_bytes=4 << 20),
        name="write_out",
    )(out, state, log)
    return out, state.reshape(tri), log.reshape(tri)


def solution(mesh):
    fault = P(("gx", "gy"))
    field = P("gx", "gy", None)
    in_specs = (field, field, P(None, "gx", "gy")) + (fault,) * 7 + (P(("gx", "gy"), None), fault)
    out_specs = (field, fault, fault)
    return jax.shard_map(local, mesh=mesh, in_specs=in_specs, out_specs=out_specs, check_vma=False)
```

```python
import functools

import jax
import jax.numpy as jnp
from jax import lax
from jax.experimental import pallas as pl
from jax.experimental.pallas import tpu as pltpu
from jax.sharding import PartitionSpec as P

SWEEPS = 3
LANES = 128
CHUNK = 16
MESH = pl.DeviceIdType.MESH

conductance = 0.15
step_time = 1.0
heal_time = 0.5
friction_ref = 0.6


def step_kernel(
    dims,
    p_hbm,
    k_hbm,
    g_hbm,
    slip_hbm,
    aging_hbm,
    normal_hbm,
    shear_hbm,
    direct_hbm,
    evolution_hbm,
    distance_hbm,
    owner_hbm,
    cell_hbm,
    out_v,
    state_ref,
    log_ref,
    p_in,
    k_in,
    g_in,
    vec_f,
    vec_i,
    root,
    u_a,
    u_b,
    coef_a,
    coef_c,
    inv,
    first_x,
    relay_x,
    later_x_send,
    later_x,
    first_y_send,
    first_y,
    later_y_send,
    later_y,
    corner_send,
    corner,
    slip_send,
    slip_part,
    slip_recv,
    req_send,
    req_recv,
    req_at,
    req_smem,
    part_send,
    part_recv,
    pick_a,
    pick_b,
    pick_n,
    pick_c,
    ans_send,
    ans_recv,
    load_sem,
    vec_sem,
    x_send,
    fx_recv,
    lx_recv,
    relay_send,
    relay_recv,
    y_send,
    y_recv,
    corner_recv,
    row_sem,
    col_sem,
    gather_ssem,
    gather_rsem,
    slip_ssem,
    slip_rsem,
    req_ssem,
    req_rsem,
    part_ssem,
    part_rsem,
    ans_ssem,
    ans_rsem,
):
    n_gx, n_gy, cx, cy, nz, tri, rows, cols, cap, cap_pad = dims
    nb = nz // LANES
    yp = cy + 8
    n_ch = cy // CHUNK
    edges = sorted({0, n_ch - 1})
    middles = [c for c in range(n_ch) if c not in edges]
    gx, gy = lax.axis_index("gx"), lax.axis_index("gy")
    lane = lax.broadcasted_iota(jnp.int32, (1, LANES), 1)

    early = (
        (owner_hbm, vec_i.at[0], vec_sem.at[0]),
        (cell_hbm, vec_i.at[1], vec_sem.at[0]),
        (slip_hbm, vec_f.at[0], vec_sem.at[1]),
    )
    late = (aging_hbm, normal_hbm, shear_hbm, direct_hbm, evolution_hbm, distance_hbm)
    half = cx // 2

    def load(which, part):
        src, dst = ((k_hbm, k_in), (p_hbm, p_in))[which]
        at = pl.ds(part * half, half)
        return pltpu.make_async_copy(src.at[at], dst.at[at], load_sem.at[which, part])

    load_g = pltpu.make_async_copy(g_hbm, g_in, vec_sem.at[3])

    barrier = pltpu.get_barrier_semaphore()

    def greet(x, y):
        pl.semaphore_signal(barrier, inc=1, device_id={"gx": x, "gy": y}, device_id_type=MESH)

    has_x = (gx > 0, gx < n_gx - 1)
    has_y = (gy > 0, gy < n_gy - 1)
    to_x = (jnp.maximum(gx - 1, 0), jnp.minimum(gx + 1, n_gx - 1))
    to_y = (jnp.maximum(gy - 1, 0), jnp.minimum(gy + 1, n_gy - 1))
    mid = n_gx // 2
    relayed = middles[:2] if n_gx >= 8 and len(middles) >= 2 else []
    is_mid = (gx == mid, gx == mid - 1)
    is_end = (gx == 0, gx == n_gx - 1)
    if relayed:
        on_relay = is_mid[0] | is_mid[1] | is_end[0] | is_end[1]
        partners = (
            jnp.where(is_end[0] | is_end[1], mid, 0),
            jnp.where(is_end[0] | is_end[1], mid - 1, n_gx - 1),
        )

    greeted = jnp.int32(0)
    for side in range(2):

        @pl.when(has_x[side])
        def _():
            greet(to_x[side], gy)

        @pl.when(has_y[side])
        def _():
            greet(gx, to_y[side])

        greeted = greeted + jnp.where(has_x[side], 1, 0) + jnp.where(has_y[side], 1, 0)
    if relayed:

        @pl.when(on_relay)
        def _():
            for partner in partners:
                greet(partner, gy)

        greeted = greeted + jnp.where(on_relay, 2, 0)

    for src, dst, sem in early:
        pltpu.make_async_copy(src, dst, sem).start()
    for part in range(2):
        for which in range(2):
            load(which, part).start()

    zero = jnp.zeros((8, LANES), jnp.float32)
    n_col = (cx + 2) * nb
    for ref in (root, u_a, u_b):
        for c in range(nb, n_col - nb + 1):
            ref[c * yp : c * yp + 8, :] = zero
        ref[0 : nb * yp, :] = jnp.zeros((nb * yp, LANES), jnp.float32)
        ref[(cx + 1) * nb * yp : (cx + 2) * nb * yp + 8, :] = jnp.zeros(
            (nb * yp + 8, LANES), jnp.float32
        )

    for ref in (pick_a, pick_b, pick_n, pick_c):
        ref[...] = jnp.zeros_like(ref)
    pl.semaphore_wait(barrier, greeted)

    def remote(src, dst, send, recv, x, y):
        return pltpu.make_async_remote_copy(
            src_ref=src,
            dst_ref=dst,
            send_sem=send,
            recv_sem=recv,
            device_id={"gx": x, "gy": y},
            device_id_type=MESH,
        )

    def first_x_copy(side, which, c):
        part = pl.ds(c * CHUNK, CHUNK)
        return remote(
            (k_hbm, p_hbm)[which].at[0 if side == 0 else cx - 1, part],
            first_x.at[1 - side, which, part],
            x_send.at[side],
            fx_recv.at[1 - side, c],
            to_x[side],
            gy,
        )

    def to_relay(side, which, i):
        part = pl.ds(relayed[i] * CHUNK, CHUNK)
        return remote(
            (k_hbm, p_hbm)[which].at[0 if side == 0 else cx - 1, part],
            relay_x.at[i, which],
            x_send.at[side],
            relay_recv.at[i],
            0 if side == 0 else n_gx - 1,
            gy,
        )

    def from_relay(side, i):
        return remote(
            relay_x.at[i],
            first_x.at[1 - side, :, pl.ds(relayed[i] * CHUNK, CHUNK)],
            relay_send,
            fx_recv.at[1 - side, relayed[i]],
            mid - 1 if side == 0 else mid,
            gy,
        )

    def pass_on(i):
        for side in range(2):

            @pl.when(is_end[side])
            def _():
                pltpu.make_async_copy(relay_x.at[i], relay_x.at[i], relay_recv.at[i]).wait()
                from_relay(side, i).start()

    def later_x_copy(turn, side, c):
        return remote(
            later_x_send.at[turn - 1, side, c],
            later_x.at[turn - 1, 1 - side, c],
            x_send.at[side],
            lx_recv.at[turn - 1, 1 - side, c],
            to_x[side],
            gy,
        )

    def landed(ref, sem):
        pltpu.make_async_copy(ref, ref, sem).wait()

    def y_copy(turn, side):
        if turn == 0:
            src, dst = first_y_send.at[side], first_y.at[1 - side]
        else:
            src, dst = later_y_send.at[turn - 1, side], later_y.at[turn - 1, 1 - side]
        return remote(src, dst, y_send.at[side], y_recv.at[turn, 1 - side], gx, to_y[side])

    def corner_copy(turn, side):
        return remote(
            corner_send.at[turn - 1, side],
            corner.at[turn - 1, 1 - side],
            y_send.at[side],
            corner_recv.at[turn - 1, 1 - side],
            gx,
            to_y[side],
        )

    for i in range(len(relayed)):
        for side in range(2):

            @pl.when(is_mid[side])
            def _():
                to_relay(side, 0, i).start()
                to_relay(side, 1, i).start()

    for c in edges + middles:
        for side in range(2):
            direct = has_x[side]
            if c in relayed:
                direct = direct & jnp.logical_not(is_mid[side])

            @pl.when(direct)
            def _():
                first_x_copy(side, 0, c).start()
                first_x_copy(side, 1, c).start()

    rounds = [], []
    for axis, size in enumerate((n_gx, n_gy)):
        reach = 1
        while reach < size - 1:
            rounds[axis].append(reach)
            reach *= 2

    def round_peers(axis, k):
        me, size, sem = ((gx, n_gx, row_sem), (gy, n_gy, col_sem))[axis]
        d = rounds[axis][k]
        low, high = jnp.maximum(me - d, 0), jnp.minimum(me + d, size - 1)
        to = [(i, gy) if axis == 0 else (gx, i) for i in (low, high)]
        return (me >= d, me + d < size), to, sem.at[k]

    def tell(axis, k):
        if k < len(rounds[axis]):
            has, to, sem = round_peers(axis, k)
            for side in range(2):

                @pl.when(has[side])
                def _():
                    pl.semaphore_signal(
                        sem,
                        inc=1,
                        device_id={"gx": to[side][0], "gy": to[side][1]},
                        device_id_type=MESH,
                    )

    def hear(axis, k):
        if k < len(rounds[axis]):
            has, _, sem = round_peers(axis, k)
            pl.semaphore_wait(sem, jnp.where(has[0], 1, 0) + jnp.where(has[1], 1, 0))

    def finish(axis, k):
        hear(axis, k)
        for later in range(k + 1, len(rounds[axis])):
            tell(axis, later)
            hear(axis, later)

    tell(1, 0)
    tell(0, 0)

    pltpu.make_async_copy(vec_i, vec_i, vec_sem.at[0]).wait()
    pltpu.make_async_copy(vec_f.at[0], vec_f.at[0], vec_sem.at[1]).wait()
    slip_send[...] = jnp.zeros_like(slip_send)
    slip_send[0, :, :tri] = vec_f[0]

    owner_row = vec_i[0]
    cell_row = vec_i[1]
    t_row = lax.broadcasted_iota(jnp.int32, (tri, tri), 1)
    t_col = lax.broadcasted_iota(jnp.int32, (tri, tri), 0)
    eye = t_row == t_col
    owner_wide = jnp.broadcast_to(owner_row, (tri, tri))
    owner_col = jnp.sum(jnp.where(eye, owner_wide, 0), axis=1, keepdims=True)
    cell_col = jnp.sum(
        jnp.where(eye, jnp.broadcast_to(cell_row, (tri, tri)), 0), axis=1, keepdims=True
    )
    same = owner_col == owner_wide
    one_below = jnp.where(same & (t_row < t_col), 1, 0)
    rank_col = jnp.sum(one_below, axis=1, keepdims=True)
    slot_col = owner_col * cap + rank_col
    width = req_send.shape[-1]
    slot_lane = lax.broadcasted_iota(jnp.int32, (tri, width), 1)
    req_send[0] = jnp.sum(jnp.where(slot_col == slot_lane, cell_col, 0), axis=0, keepdims=True)
    req_recv[pl.ds(gx, 1)] = req_send[...]

    def prepare(x, _):
        for j in range(nb):
            k = k_in[x, :, j * LANES : (j + 1) * LANES]
            p = p_in[x, :, j * LANES : (j + 1) * LANES]
            r = lax.rsqrt(k)
            s = k * r
            at = pl.ds(pl.multiple_of(((x + 1) * nb + j) * yp + 8, 8), cy)
            dense = pl.ds(pl.multiple_of((x * nb + j) * cy, 8), cy)
            root[at, :] = s
            u_a[at, :] = s * p
            inv[dense, :] = r
            coef_c[dense, :] = conductance * k
        return 0

    for part in range(2):
        load(0, part).wait()
        load(1, part).wait()
        lax.fori_loop(part * half, (part + 1) * half, prepare, 0)
    load_g.start()
    for i, src in enumerate(late):
        pltpu.make_async_copy(src, vec_f.at[1 + i], vec_sem.at[2]).start()

    n_face = cx * nb

    def face(y):
        return pl.ds(nb * yp + 8 + y, n_face, stride=yp)

    def dense_face(y):
        return pl.ds(y, n_face, stride=cy)

    y_of = (0, cy - 1)
    for side in range(2):
        first_y_send[side, 0] = root[face(y_of[side]), :]
        first_y_send[side, 1] = u_a[face(y_of[side]), :]
    for side in range(2):

        @pl.when(has_y[side])
        def _():
            y_copy(0, side).start()

    def around(ref, x, y0):
        here, sums = [], []
        for j in range(nb):
            at = ((x + 1) * nb + j) * yp + 8 + y0
            here.append(ref[at : at + CHUNK, :])
        for j in range(nb):
            at = ((x + 1) * nb + j) * yp + 8 + y0
            before = here[j - 1] if j > 0 else 0.0
            after = here[j + 1] if j < nb - 1 else 0.0
            left = pltpu.roll(jnp.where(lane == LANES - 1, before, here[j]), 1, 1)
            right = pltpu.roll(jnp.where(lane == 0, after, here[j]), LANES - 1, 1)
            step = nb * yp
            total = ref[at + step : at + step + CHUNK, :] + ref[at - step : at - step + CHUNK, :]
            total = total + (ref[at + 1 : at + 1 + CHUNK, :] + ref[at - 1 : at - 1 + CHUNK, :])
            sums.append(total + (left + right))
        return here, sums

    def sweep(turn, src, dst, planes, chunks):
        for x in planes:
            for c in chunks:
                y0 = c * CHUNK
                here, sums = around(src, x, y0)
                if turn == 0:
                    roots, root_sums = around(root, x, y0)
                for j in range(nb):
                    at = ((x + 1) * nb + j) * yp + 8 + y0
                    dense = (x * nb + j) * cy + y0
                    if turn == 0:
                        a = 1.0 - conductance * (roots[j] * root_sums[j])
                        coef_a[dense : dense + CHUNK, :] = a
                    else:
                        a = coef_a[dense : dense + CHUNK, :]
                    new = a * here[j] + coef_c[dense : dense + CHUNK, :] * sums[j]
                    if turn < SWEEPS - 1:
                        dst[at : at + CHUNK, :] = new
                    else:
                        out_v[x, y0 : y0 + CHUNK, j * LANES : (j + 1) * LANES] = (
                            new * inv[dense : dense + CHUNK, :]
                        )

    def fix_x(turn, side, c, src, dst):
        x = 0 if side == 0 else cx - 1
        y0 = c * CHUNK
        for j in range(nb):
            at = pl.ds(((x + 1) * nb + j) * yp + 8 + y0, CHUNK)
            dense = pl.ds((x * nb + j) * cy + y0, CHUNK)
            part = slice(j * CHUNK, (j + 1) * CHUNK)
            ys, zs = slice(y0, y0 + CHUNK), slice(j * LANES, (j + 1) * LANES)
            if turn == 0:
                k = first_x[side, 0, ys, zs]
                s = k * lax.rsqrt(k)
                halo = s * first_x[side, 1, ys, zs]
                less = conductance * (root[at, :] * s)
                coef_a[dense, :] = coef_a[dense, :] - less
                new = dst[at, :] + (coef_c[dense, :] * halo - less * src[at, :])
            else:
                halo = later_x[turn - 1, side, c, part, :]
                if turn < SWEEPS - 1:
                    new = dst[at, :] + coef_c[dense, :] * halo
            if turn < SWEEPS - 1:
                dst[at, :] = new
                later_x_send[turn, side, c, part, :] = new
            else:
                out_v[x, ys, zs] = out_v[x, ys, zs] + coef_c[dense, :] * inv[dense, :] * halo

    def take_x(turn, c, src, dst):
        for side in range(2):

            @pl.when(has_x[side])
            def _():
                if turn == 0:
                    landed(first_x.at[side, :, pl.ds(c * CHUNK, CHUNK)], fx_recv.at[side, c])
                else:
                    landed(later_x.at[turn - 1, side, c], lx_recv.at[turn - 1, side, c])
                fix_x(turn, side, c, src, dst)
                if turn < SWEEPS - 1:
                    later_x_copy(turn + 1, side, c).start()

    n_inner = (cx - 4) * nb

    def inner_face(y):
        return pl.ds(3 * nb * yp + 8 + y, n_inner, stride=yp)

    def inner_dense(y):
        return pl.ds(2 * nb * cy + y, n_inner, stride=cy)

    def corner_faces(y):
        for i, x in enumerate((0, cx - 2)):
            yield (
                pl.ds((x + 1) * nb * yp + 8 + y, 2 * nb, stride=yp),
                pl.ds(x * nb * cy + y, 2 * nb, stride=cy),
                slice(2 * i * nb, 2 * (i + 1) * nb),
            )

    def take_y(turn, src, dst):
        for side in range(2):

            @pl.when(has_y[side])
            def _():
                if turn == 0:
                    landed(first_y.at[side], y_recv.at[turn, side])
                    at, dense = face(y_of[side]), dense_face(y_of[side])
                    s, halo = first_y[side, 0], first_y[side, 1]
                    less = conductance * (root[at, :] * s)
                    coef_a[dense, :] = coef_a[dense, :] - less
                    dst[at, :] = dst[at, :] + (coef_c[dense, :] * halo - less * src[at, :])
                else:
                    landed(later_y.at[turn - 1, side], y_recv.at[turn, side])
                    if turn < SWEEPS - 1:
                        at, dense = inner_face(y_of[side]), inner_dense(y_of[side])
                        dst[at, :] = dst[at, :] + coef_c[dense, :] * later_y[turn - 1, side]
                    else:
                        src[inner_face(-1 if side == 0 else cy), :] = later_y[turn - 1, side]

    def take_corner(turn, src, dst):
        for side in range(2):

            @pl.when(has_y[side])
            def _():
                landed(corner.at[turn - 1, side], corner_recv.at[turn - 1, side])
                if turn < SWEEPS - 1:
                    for at, dense, part in corner_faces(y_of[side]):
                        dst[at, :] = dst[at, :] + coef_c[dense, :] * corner[turn - 1, side, part, :]
                else:
                    for at, _, part in corner_faces(-1 if side == 0 else cy):
                        src[at, :] = corner[turn - 1, side, part, :]

    def send_y(turn, ref):
        for side in range(2):

            @pl.when(has_y[side])
            def _():
                later_y_send[turn - 1, side] = ref[inner_face(y_of[side]), :]
                y_copy(turn, side).start()

    def send_corner(turn, ref):
        for side in range(2):

            @pl.when(has_y[side])
            def _():
                for at, _, part in corner_faces(y_of[side]):
                    corner_send[turn - 1, side, part, :] = ref[at, :]
                corner_copy(turn, side).start()

    every = list(range(n_ch))
    inner, outer = range(2, cx - 2), (0, 1, cx - 2, cx - 1)
    per = n_gx // n_gy
    home = gx // per
    share = gx % per

    def gather_copy():
        return remote(slip_send.at[0], slip_part.at[gy], gather_ssem, gather_rsem, gx, home)

    def gather_slip():
        @pl.when(home != gy)
        def _():
            gather_copy().start()

        @pl.when(home == gy)
        def _():
            slip_part[pl.ds(gy, 1)] = slip_send[...]

    def gather_when(mine):
        @pl.when(mine)
        def _():
            finish(1, 1)
            gather_slip()

    quarter = cx // 4
    late_x = (gx == n_gx // 2) | (gx == n_gx // 2 - 1)
    sweep(0, u_a, u_b, range(quarter), every)
    for axis in (1, 0):
        hear(axis, 0)
        tell(axis, 1)
    sweep(0, u_a, u_b, range(quarter, 2 * quarter), every)
    gather_when(gx == 0)
    if relayed:
        pass_on(0)
    sweep(0, u_a, u_b, range(2 * quarter, 3 * quarter), every)
    gather_when((gx > 0) & jnp.logical_not(late_x))
    for i in range(1, len(relayed)):
        pass_on(i)
    sweep(0, u_a, u_b, range(3 * quarter, cx), every)

    def req_copy(off):
        return remote(
            req_send.at[0], req_recv.at[gx], req_ssem, req_rsem, (gx + off) % n_gx, gy
        )


    def slip_copy(off):
        part = pl.ds(share * n_gy, n_gy)
        return remote(
            slip_part.at[pl.ds(0, n_gy)], slip_recv.at[part], slip_ssem, slip_rsem, (gx + off) % n_gx, gy
        )

    def spread_slip():
        @pl.when(home == gy)
        def _():
            landed(slip_part.at[pl.ds(0, n_gy - 1)], gather_rsem)
            for off in range(1, n_gx):
                slip_copy(off).start()
            slip_recv[pl.ds(share * n_gy, n_gy)] = slip_part[:n_gy]

    take_y(0, u_a, u_b)
    send_y(1, u_b)
    hear(0, 1)
    tell(0, 2)
    for c in edges:
        take_x(0, c, u_a, u_b)
    send_corner(1, u_b)
    gather_when((gx > 0) & late_x)
    sweep(1, u_b, u_a, inner, every)
    finish(0, 2)
    for off in range(1, n_gx):
        req_copy(off).start()

    def next_y(mine):
        @pl.when(mine)
        def _():
            take_y(1, u_b, u_a)
            send_y(2, u_a)

    next_y(late_x)
    for c in middles:
        take_x(0, c, u_a, u_b)
    spread_slip()
    sweep(1, u_b, u_a, outer, every)
    next_y(jnp.logical_not(late_x))

    take_corner(1, u_b, u_a)
    for c in edges:
        take_x(1, c, u_b, u_a)
    send_corner(2, u_a)
    if middles:
        sweep(2, u_a, None, inner, middles)

    landed(req_recv.at[pl.ds(0, n_gx - 1)], req_rsem)
    asked = pltpu.roll(req_recv[...], (width + (1 - gx) * cap) % width, 2)
    at_x, in_x = part_of(asked, cy * nz), rest_of(asked, cy * nz)
    at_y, at_z = part_of(in_x, nz), rest_of(in_x, nz)
    at_j, at_l = part_of(at_z, LANES), rest_of(at_z, LANES)
    slot_at = lax.broadcasted_iota(jnp.int32, asked.shape, 2)
    above, below = slot_at >= 2 * cap, slot_at < cap
    req_at[0] = ((at_x + 1) * nb + at_j) * yp + 8 + at_y
    req_at[1] = (at_x * nb + at_j) * cy + at_y
    req_at[2] = at_l
    req_at[3] = jnp.where(at_z == 0, -1, at_l + (LANES - 1))
    req_at[4] = jnp.where(at_z == nz - 1, -1, at_l - (LANES - 1))
    req_at[5] = (jnp.where(above, cx, 1) * nb + at_j) * yp + 8 + at_y
    req_at[6] = jnp.where((above & (at_x == 0)) | (below & (at_x == cx - 1)), at_l, -1)
    to_smem = pltpu.make_async_copy(req_at, req_smem, vec_sem.at[0])
    to_smem.start()

    landed(vec_f.at[pl.ds(1, len(late))], vec_sem.at[2])
    distance = vec_f[6]
    ratio = distance / vec_f[0]
    state_next = ratio + (vec_f[1] - ratio) * jnp.exp(-heal_time / ratio)
    state_ref[...] = state_next
    evolved = vec_f[5] * jnp.log(state_next / distance)

    @pl.when(home != gy)
    def _():
        landed(slip_recv.at[pl.ds(0, per * n_gy)], slip_rsem)

    if per > 1:

        @pl.when(home == gy)
        def _():
            landed(slip_recv.at[pl.ds(0, (per - 1) * n_gy)], slip_rsem)

    load_g.wait()
    n_cb = cols // LANES
    segment = [jnp.zeros((1, LANES), jnp.float32) for _ in range(n_cb)]
    for i in range(n_gx):
        first, shift = (i * tri) // LANES, (i * tri) % LANES
        row = slip_recv[i]
        if shift:
            row = pltpu.roll(row, shift, 1)
        segment[first] = segment[first] + jnp.where(lane >= shift, row, 0.0)
        if shift + tri > LANES:
            segment[first + 1] = segment[first + 1] + jnp.where(lane < shift, row, 0.0)
    eye_f = lax.broadcasted_iota(jnp.int32, (tri, LANES), 0) == lax.broadcasted_iota(
        jnp.int32, (tri, LANES), 1
    )
    for part in range(n_gy):
        for comp in range(2):
            total = jnp.zeros((tri, LANES), jnp.float32)
            for b in range(n_cb):
                block = g_in[comp, part * tri : (part + 1) * tri, b * LANES : (b + 1) * LANES]
                total = total + block * segment[b]
            sums = jnp.sum(total, axis=1, keepdims=True)
            part_send[part, comp : comp + 1, :] = jnp.sum(
                jnp.where(eye_f, sums, 0.0), axis=0, keepdims=True
            )

    def part_copy(off):
        to = (gy + off) % n_gy
        return remote(
            part_send.at[to], part_recv.at[gy], part_ssem, part_rsem, gx, to
        )

    part_recv[pl.ds(gy, 1)] = part_send[pl.ds(gy, 1)]
    for off in range(1, n_gy):
        part_copy(off).start()


    for c in middles:
        take_x(1, c, u_b, u_a)
    to_smem.wait()

    def across(source, _):
        for s in range(2 * cap):
            slot = s if s < cap else cap + s
            row = u_a[pl.ds(req_smem[5, source, 0, slot], 1), :]
            pick_c[source, s : s + 1, :] = jnp.where(
                lane == req_smem[6, source, 0, slot], row, 0.0
            )
        return 0

    lax.fori_loop(0, n_gx, across, 0)
    take_y(2, u_a, None)
    take_corner(2, u_a, None)

    def answer(source, _):
        for s in range(cap):
            slot = cap + s
            at = req_smem[0, source, 0, slot]
            dense = pl.ds(req_smem[1, source, 0, slot], 1)
            z = req_smem[2, source, 0, slot]
            here = u_a[pl.ds(at, 1), :]
            step = nb * yp
            beside = (u_a[pl.ds(at + step, 1), :] + u_a[pl.ds(at - step, 1), :]) + (
                u_a[pl.ds(at + 1, 1), :] + u_a[pl.ds(at - 1, 1), :]
            )
            near = jnp.where((lane == z - 1) | (lane == z + 1), here, 0.0)
            near = near + jnp.where(
                lane == req_smem[3, source, 0, slot], u_a[pl.ds(at - yp, 1), :], 0.0
            )
            near = near + jnp.where(
                lane == req_smem[4, source, 0, slot], u_a[pl.ds(at + yp, 1), :], 0.0
            )
            back = inv[dense, :]
            weight = coef_c[dense, :] * back
            pick_a[source, s : s + 1, :] = jnp.where(
                lane == z, (coef_a[dense, :] * here) * back + weight * beside, 0.0
            )
            pick_b[source, s : s + 1, :] = jnp.where(lane == z, weight, 0.0)
            pick_n[source, s : s + 1, :] = near
        return 0

    lax.fori_loop(0, n_gx, answer, 0)

    def spread(values, first):
        n = values.shape[1]
        to_lane = lax.broadcasted_iota(jnp.int32, (n_gx, n, width), 2)
        of_slot = lax.broadcasted_iota(jnp.int32, (n_gx, n, width), 1)
        return jnp.sum(jnp.where(to_lane == first(of_slot), values, 0.0), axis=1, keepdims=True)

    def own(slot):
        return jnp.where(slot < cap, gx * cap + slot, -1)

    def beyond(slot):
        lane_of = jnp.where(slot < cap, (gx - 1) * cap + slot, gx * cap + slot)
        return jnp.where(slot < 2 * cap, lane_of, -1)

    weights = jnp.sum(pick_b[...], axis=2, keepdims=True)
    values = jnp.sum(pick_a[...], axis=2, keepdims=True) + weights * jnp.sum(
        pick_n[...], axis=2, keepdims=True
    )
    ans_send[:, 0] = spread(values, own)
    ans_send[:, 1] = spread(weights, own)
    ans_send[:, 2] = spread(jnp.sum(pick_c[...], axis=2, keepdims=True), beyond)

    def ans_copy(off):
        to = (gx + off) % n_gx
        return remote(
            ans_send.at[to], ans_recv.at[gx], ans_ssem, ans_rsem, to, gy
        )

    for off in range(1, n_gx):
        ans_copy(off).start()
    ans_recv[pl.ds(gx, 1)] = ans_send[pl.ds(gx, 1)]

    sweep(2, u_a, None, inner, edges)
    sweep(2, u_a, None, outer, every)
    for c in edges + middles:
        take_x(2, c, u_a, None)

    landed(ans_recv.at[pl.ds(0, n_gx - 1)], ans_rsem)
    answers = [ans_recv[0, i] for i in range(3)]
    for other in range(1, n_gx):
        answers = [answers[i] + ans_recv[other, i] for i in range(3)]
    answers = answers[0] + answers[1] * answers[2]
    found = jnp.sum(jnp.where(slot_col == slot_lane, answers, 0.0), axis=1, keepdims=True)
    fault = jnp.sum(jnp.where(eye, found, 0.0), axis=0, keepdims=True)
    landed(part_recv.at[pl.ds(0, n_gy - 1)], part_rsem)
    rates = part_recv[0]
    for other in range(1, n_gy):
        rates = rates + part_recv[other]
    shear = vec_f[3] + step_time * rates[0:1, :tri]
    loaded = vec_f[2] + step_time * rates[1:2, :tri]
    log_ref[...] = (shear / (loaded - fault) - friction_ref - evolved) / vec_f[4]

    for side in range(2):

        @pl.when(has_x[side])
        def _():
            landed(p_in.at[pl.ds(0, SWEEPS + 1)], x_send.at[side])

        @pl.when(has_y[side])
        def _():
            landed(coef_a.at[pl.ds(0, (SWEEPS + 1) * n_face)], y_send.at[side])

        if relayed:

            @pl.when(is_end[side])
            def _():
                landed(relay_x.at[pl.ds(0, len(relayed))], relay_send)

    @pl.when(home != gy)
    def _():
        gather_copy().wait_send()

    @pl.when(home == gy)
    def _():
        landed(slip_part, slip_ssem)

    landed(req_recv.at[pl.ds(0, n_gx - 1)], req_ssem)
    landed(ans_recv.at[pl.ds(0, n_gx - 1)], ans_ssem)
    landed(part_recv.at[pl.ds(0, n_gy - 1)], part_ssem)


def part_of(value, size):
    if size & (size - 1) == 0:
        return lax.shift_right_logical(value, jnp.int32(size.bit_length() - 1))
    return lax.div(value, jnp.int32(size))


def rest_of(value, size):
    if size & (size - 1) == 0:
        return value & (size - 1)
    return lax.rem(value, jnp.int32(size))


def write_kernel(p_ref, state_in, log_in, out_hbm, state_hbm, log_hbm, sem):
    planes = p_ref.shape[0]
    n = 4 if planes % 4 == 0 else 1
    for i in range(n):
        part = pl.ds(i * planes // n, planes // n)
        pltpu.make_async_copy(p_ref.at[part], out_hbm.at[part], sem.at[0]).start()
    small = [
        pltpu.make_async_copy(state_in, state_hbm, sem.at[1]),
        pltpu.make_async_copy(log_in, log_hbm, sem.at[2]),
    ]
    for copy in small:
        copy.start()
    pltpu.make_async_copy(p_ref, out_hbm, sem.at[0]).wait()
    for copy in small:
        copy.wait()


def local(
    pressure,
    permeability,
    kernel,
    slip_rate,
    aging_state,
    normal_stress,
    shear_stress,
    direct_effect,
    evolution_effect,
    slip_distance,
    tri_owner,
    tri_cell,
):
    n_gx, n_gy = lax.axis_size("gx"), lax.axis_size("gy")
    cx, cy, nz = pressure.shape
    tri = slip_rate.shape[0]
    _, rows, cols = kernel.shape
    cap = max(2, 2 * tri // n_gx)
    cap_pad = -(-cap // 8) * 8
    nb = nz // LANES
    yp = cy + 8
    n_ch = cy // CHUNK
    padded = ((cx + 2) * nb * yp + 8, LANES)
    dense = (cx * nb * cy, LANES)
    width = -(-n_gx * cap // LANES) * LANES
    dims = (n_gx, n_gy, cx, cy, nz, tri, rows, cols, cap, cap_pad)
    f32, i32 = jnp.float32, jnp.int32
    dma = pltpu.SemaphoreType.DMA
    hbm = lambda a: pltpu.with_memory_space_constraint(a, pltpu.HBM)
    vec = lambda a: hbm(a.reshape(1, tri))
    any_spec = pl.BlockSpec(memory_space=pl.ANY)
    hbm_spec = pl.BlockSpec(memory_space=pltpu.HBM)
    vmem_spec = pl.BlockSpec(memory_space=pltpu.VMEM)
    out, state, log = pl.pallas_call(
        functools.partial(step_kernel, dims),
        out_shape=(
            pltpu.VMEM(pressure.shape, f32),
            pltpu.VMEM((1, tri), f32),
            pltpu.VMEM((1, tri), f32),
        ),
        in_specs=[hbm_spec] * 12,
        out_specs=(vmem_spec, vmem_spec, vmem_spec),
        scratch_shapes=[
            pltpu.VMEM(pressure.shape, f32),
            pltpu.VMEM(pressure.shape, f32),
            pltpu.VMEM(kernel.shape, f32),
            pltpu.VMEM((7, 1, tri), f32),
            pltpu.VMEM((2, 1, tri), i32),
            pltpu.VMEM(padded, f32),
            pltpu.VMEM(padded, f32),
            pltpu.VMEM(padded, f32),
            pltpu.VMEM(dense, f32),
            pltpu.VMEM(dense, f32),
            pltpu.VMEM(dense, f32),
            pltpu.VMEM((2, 2, cy, nz), f32),
            pltpu.VMEM((2, 2, CHUNK, nz), f32),
            pltpu.VMEM((SWEEPS - 1, 2, n_ch, nb * CHUNK, LANES), f32),
            pltpu.VMEM((SWEEPS - 1, 2, n_ch, nb * CHUNK, LANES), f32),
            pltpu.VMEM((2, 2, cx * nb, LANES), f32),
            pltpu.VMEM((2, 2, cx * nb, LANES), f32),
            pltpu.VMEM((SWEEPS - 1, 2, (cx - 4) * nb, LANES), f32),
            pltpu.VMEM((SWEEPS - 1, 2, (cx - 4) * nb, LANES), f32),
            pltpu.VMEM((SWEEPS - 1, 2, 4 * nb, LANES), f32),
            pltpu.VMEM((SWEEPS - 1, 2, 4 * nb, LANES), f32),
            pltpu.VMEM((1, 1, LANES), f32),
            pltpu.VMEM((n_gy * (n_gx - 1), 1, LANES), f32),
            pltpu.VMEM((n_gx, 1, LANES), f32),
            pltpu.VMEM((1, 1, width), i32),
            pltpu.VMEM((n_gx, 1, width), i32),
            pltpu.VMEM((7, n_gx, 1, width), i32),
            pltpu.SMEM((7, n_gx, 1, width), i32),
            pltpu.VMEM((n_gy, 2, LANES), f32),
            pltpu.VMEM((n_gy, 2, LANES), f32),
            pltpu.VMEM((n_gx, cap_pad, LANES), f32),
            pltpu.VMEM((n_gx, cap_pad, LANES), f32),
            pltpu.VMEM((n_gx, cap_pad, LANES), f32),
            pltpu.VMEM((n_gx, -(-2 * cap // 8) * 8, LANES), f32),
            pltpu.VMEM((n_gx, 3, 1, width), f32),
            pltpu.VMEM((n_gx, 3, 1, width), f32),
            dma((2, 2)),
            dma((4,)),
            dma((2,)),
            dma((2, n_ch)),
            dma((SWEEPS - 1, 2, n_ch)),
            dma,
            dma((2,)),
            dma((2,)),
            dma((SWEEPS, 2)),
            dma((SWEEPS - 1, 2)),
            pltpu.SemaphoreType.REGULAR((max(1, (n_gx - 2).bit_length()),)),
            pltpu.SemaphoreType.REGULAR((max(1, (n_gy - 2).bit_length()),)),
            dma,
            dma,
            dma,
            dma,
            dma,
            dma,
            dma,
            dma,
            dma,
            dma,
        ],
        compiler_params=pltpu.CompilerParams(
            collective_id=0, has_side_effects=True, vmem_limit_bytes=40 << 20
        ),
        name="fault_step",
    )(
        hbm(pressure),
        hbm(permeability),
        hbm(kernel),
        vec(slip_rate),
        vec(aging_state),
        vec(normal_stress),
        vec(shear_stress),
        vec(direct_effect),
        vec(evolution_effect),
        vec(slip_distance),
        vec(tri_owner),
        vec(tri_cell),
    )
    out, state, log = pl.pallas_call(
        write_kernel,
        out_shape=(
            jax.ShapeDtypeStruct(pressure.shape, f32),
            jax.ShapeDtypeStruct((1, tri), f32),
            jax.ShapeDtypeStruct((1, tri), f32),
        ),
        in_specs=[vmem_spec] * 3,
        out_specs=(any_spec,) * 3,
        scratch_shapes=[dma((3,))],
        compiler_params=pltpu.CompilerParams(vmem_limit_bytes=4 << 20),
        name="write_out",
    )(out, state, log)
    return out, state.reshape(tri), log.reshape(tri)


def solution(mesh):
    fault = P(("gx", "gy"))
    field = P("gx", "gy", None)
    in_specs = (field, field, P(None, "gx", "gy")) + (fault,) * 7 + (P(("gx", "gy"), None), fault)
    out_specs = (field, fault, fault)
    return jax.shard_map(local, mesh=mesh, in_specs=in_specs, out_specs=out_specs, check_vma=False)
```

```python
import functools

import jax
import jax.numpy as jnp
from jax import lax
from jax.experimental import pallas as pl
from jax.experimental.pallas import tpu as pltpu
from jax.sharding import PartitionSpec as P

SWEEPS = 3
LANES = 128
CHUNK = 16
MESH = pl.DeviceIdType.MESH

conductance = 0.15
step_time = 1.0
heal_time = 0.5
friction_ref = 0.6


def step_kernel(
    dims,
    p_hbm,
    k_hbm,
    g_hbm,
    slip_hbm,
    aging_hbm,
    normal_hbm,
    shear_hbm,
    direct_hbm,
    evolution_hbm,
    distance_hbm,
    owner_hbm,
    cell_hbm,
    out_v,
    state_ref,
    log_ref,
    p_in,
    k_in,
    g_in,
    vec_f,
    vec_i,
    root,
    u_a,
    u_b,
    coef_a,
    coef_c,
    inv,
    first_x,
    relay_x,
    later_x_send,
    later_x,
    first_y_send,
    first_y,
    later_y_send,
    later_y,
    corner_send,
    corner,
    slip_send,
    slip_part,
    slip_recv,
    req_send,
    req_recv,
    req_at,
    req_smem,
    part_send,
    part_recv,
    pick_a,
    pick_b,
    pick_n,
    pick_c,
    ans_send,
    ans_recv,
    load_sem,
    vec_sem,
    x_send,
    fx_recv,
    lx_recv,
    relay_send,
    relay_recv,
    y_send,
    y_recv,
    corner_recv,
    row_sem,
    col_sem,
    gather_ssem,
    gather_rsem,
    slip_ssem,
    slip_rsem,
    req_ssem,
    req_rsem,
    part_ssem,
    part_rsem,
    ans_ssem,
    ans_rsem,
):
    n_gx, n_gy, cx, cy, nz, tri, rows, cols, cap, cap_pad = dims
    nb = nz // LANES
    yp = cy + 8
    n_ch = cy // CHUNK
    edges = sorted({0, n_ch - 1})
    middles = [c for c in range(n_ch) if c not in edges]
    gx, gy = lax.axis_index("gx"), lax.axis_index("gy")
    lane = lax.broadcasted_iota(jnp.int32, (1, LANES), 1)

    early = (
        (owner_hbm, vec_i.at[0], vec_sem.at[0]),
        (cell_hbm, vec_i.at[1], vec_sem.at[0]),
        (slip_hbm, vec_f.at[0], vec_sem.at[1]),
    )
    late = (aging_hbm, normal_hbm, shear_hbm, direct_hbm, evolution_hbm, distance_hbm)
    half = cx // 2

    def load(which, part):
        src, dst = ((k_hbm, k_in), (p_hbm, p_in))[which]
        at = pl.ds(part * half, half)
        return pltpu.make_async_copy(src.at[at], dst.at[at], load_sem.at[part])

    load_g = pltpu.make_async_copy(g_hbm, g_in, vec_sem.at[3])

    barrier = pltpu.get_barrier_semaphore()

    def greet(x, y):
        pl.semaphore_signal(barrier, inc=1, device_id={"gx": x, "gy": y}, device_id_type=MESH)

    has_x = (gx > 0, gx < n_gx - 1)
    has_y = (gy > 0, gy < n_gy - 1)
    to_x = (jnp.maximum(gx - 1, 0), jnp.minimum(gx + 1, n_gx - 1))
    to_y = (jnp.maximum(gy - 1, 0), jnp.minimum(gy + 1, n_gy - 1))
    mid = n_gx // 2
    relayed = middles[:2] if n_gx >= 8 and len(middles) >= 2 else []
    is_mid = (gx == mid, gx == mid - 1)
    is_end = (gx == 0, gx == n_gx - 1)
    if relayed:
        on_relay = is_mid[0] | is_mid[1] | is_end[0] | is_end[1]
        partners = (
            jnp.where(is_end[0] | is_end[1], mid, 0),
            jnp.where(is_end[0] | is_end[1], mid - 1, n_gx - 1),
        )

    greeted = jnp.int32(0)
    for side in range(2):

        @pl.when(has_x[side])
        def _():
            greet(to_x[side], gy)

        @pl.when(has_y[side])
        def _():
            greet(gx, to_y[side])

        greeted = greeted + jnp.where(has_x[side], 1, 0) + jnp.where(has_y[side], 1, 0)
    if relayed:

        @pl.when(on_relay)
        def _():
            for partner in partners:
                greet(partner, gy)

        greeted = greeted + jnp.where(on_relay, 2, 0)

    for src, dst, sem in early:
        pltpu.make_async_copy(src, dst, sem).start()
    for part in range(2):
        for which in range(2):
            load(which, part).start()

    zero = jnp.zeros((8, LANES), jnp.float32)
    n_col = (cx + 2) * nb
    for ref in (root, u_a, u_b):
        for c in range(nb, n_col - nb + 1):
            ref[c * yp : c * yp + 8, :] = zero
        ref[0 : nb * yp, :] = jnp.zeros((nb * yp, LANES), jnp.float32)
        ref[(cx + 1) * nb * yp : (cx + 2) * nb * yp + 8, :] = jnp.zeros(
            (nb * yp + 8, LANES), jnp.float32
        )

    for ref in (pick_a, pick_b, pick_n, pick_c):
        ref[...] = jnp.zeros_like(ref)
    pl.semaphore_wait(barrier, greeted)

    def remote(src, dst, send, recv, x, y):
        return pltpu.make_async_remote_copy(
            src_ref=src,
            dst_ref=dst,
            send_sem=send,
            recv_sem=recv,
            device_id={"gx": x, "gy": y},
            device_id_type=MESH,
        )

    def first_x_copy(side, which, c):
        part = pl.ds(c * CHUNK, CHUNK)
        return remote(
            (k_hbm, p_hbm)[which].at[0 if side == 0 else cx - 1, part],
            first_x.at[1 - side, which, part],
            x_send.at[side],
            fx_recv.at[1 - side, c],
            to_x[side],
            gy,
        )

    def to_relay(side, which, i):
        part = pl.ds(relayed[i] * CHUNK, CHUNK)
        return remote(
            (k_hbm, p_hbm)[which].at[0 if side == 0 else cx - 1, part],
            relay_x.at[i, which],
            x_send.at[side],
            relay_recv.at[i],
            0 if side == 0 else n_gx - 1,
            gy,
        )

    def from_relay(side, i):
        return remote(
            relay_x.at[i],
            first_x.at[1 - side, :, pl.ds(relayed[i] * CHUNK, CHUNK)],
            relay_send,
            fx_recv.at[1 - side, relayed[i]],
            mid - 1 if side == 0 else mid,
            gy,
        )

    def pass_on(i):
        for side in range(2):

            @pl.when(is_end[side])
            def _():
                pltpu.make_async_copy(relay_x.at[i], relay_x.at[i], relay_recv.at[i]).wait()
                from_relay(side, i).start()

    def later_x_copy(turn, side, c):
        return remote(
            later_x_send.at[turn - 1, side, c],
            later_x.at[turn - 1, 1 - side, c],
            x_send.at[side],
            lx_recv.at[turn - 1, 1 - side, c],
            to_x[side],
            gy,
        )

    def landed(ref, sem):
        pltpu.make_async_copy(ref, ref, sem).wait()

    def y_copy(turn, side):
        if turn == 0:
            src, dst = first_y_send.at[side], first_y.at[1 - side]
        else:
            src, dst = later_y_send.at[turn - 1, side], later_y.at[turn - 1, 1 - side]
        return remote(src, dst, y_send.at[side], y_recv.at[turn, 1 - side], gx, to_y[side])

    def corner_copy(turn, side):
        return remote(
            corner_send.at[turn - 1, side],
            corner.at[turn - 1, 1 - side],
            y_send.at[side],
            corner_recv.at[turn - 1, 1 - side],
            gx,
            to_y[side],
        )

    for i in range(len(relayed)):
        for side in range(2):

            @pl.when(is_mid[side])
            def _():
                to_relay(side, 0, i).start()
                to_relay(side, 1, i).start()

    for c in edges + middles:
        for side in range(2):
            direct = has_x[side]
            if c in relayed:
                direct = direct & jnp.logical_not(is_mid[side])

            @pl.when(direct)
            def _():
                first_x_copy(side, 0, c).start()
                first_x_copy(side, 1, c).start()

    rounds = [], []
    for axis, size in enumerate((n_gx, n_gy)):
        reach = 1
        while reach < size - 1:
            rounds[axis].append(reach)
            reach *= 2

    def round_peers(axis, k):
        me, size, sem = ((gx, n_gx, row_sem), (gy, n_gy, col_sem))[axis]
        d = rounds[axis][k]
        low, high = jnp.maximum(me - d, 0), jnp.minimum(me + d, size - 1)
        to = [(i, gy) if axis == 0 else (gx, i) for i in (low, high)]
        return (me >= d, me + d < size), to, sem.at[k]

    def tell(axis, k):
        if k < len(rounds[axis]):
            has, to, sem = round_peers(axis, k)
            for side in range(2):

                @pl.when(has[side])
                def _():
                    pl.semaphore_signal(
                        sem,
                        inc=1,
                        device_id={"gx": to[side][0], "gy": to[side][1]},
                        device_id_type=MESH,
                    )

    def hear(axis, k):
        if k < len(rounds[axis]):
            has, _, sem = round_peers(axis, k)
            pl.semaphore_wait(sem, jnp.where(has[0], 1, 0) + jnp.where(has[1], 1, 0))

    def finish(axis, k):
        hear(axis, k)
        for later in range(k + 1, len(rounds[axis])):
            tell(axis, later)
            hear(axis, later)

    tell(1, 0)
    tell(0, 0)

    pltpu.make_async_copy(vec_i, vec_i, vec_sem.at[0]).wait()
    pltpu.make_async_copy(vec_f.at[0], vec_f.at[0], vec_sem.at[1]).wait()
    slip_send[...] = jnp.zeros_like(slip_send)
    slip_send[0, :, :tri] = vec_f[0]

    owner_row = vec_i[0]
    cell_row = vec_i[1]
    t_row = lax.broadcasted_iota(jnp.int32, (tri, tri), 1)
    t_col = lax.broadcasted_iota(jnp.int32, (tri, tri), 0)
    eye = t_row == t_col
    owner_wide = jnp.broadcast_to(owner_row, (tri, tri))
    owner_col = jnp.sum(jnp.where(eye, owner_wide, 0), axis=1, keepdims=True)
    cell_col = jnp.sum(
        jnp.where(eye, jnp.broadcast_to(cell_row, (tri, tri)), 0), axis=1, keepdims=True
    )
    same = owner_col == owner_wide
    one_below = jnp.where(same & (t_row < t_col), 1, 0)
    rank_col = jnp.sum(one_below, axis=1, keepdims=True)
    slot_col = owner_col * cap + rank_col
    width = req_send.shape[-1]
    slot_lane = lax.broadcasted_iota(jnp.int32, (tri, width), 1)
    req_send[0] = jnp.sum(jnp.where(slot_col == slot_lane, cell_col, 0), axis=0, keepdims=True)
    req_recv[pl.ds(gx, 1)] = req_send[...]

    def prepare(x, _):
        for j in range(nb):
            k = k_in[x, :, j * LANES : (j + 1) * LANES]
            p = p_in[x, :, j * LANES : (j + 1) * LANES]
            r = lax.rsqrt(k)
            s = k * r
            at = pl.ds(pl.multiple_of(((x + 1) * nb + j) * yp + 8, 8), cy)
            dense = pl.ds(pl.multiple_of((x * nb + j) * cy, 8), cy)
            root[at, :] = s
            u_a[at, :] = s * p
            inv[dense, :] = r
            coef_c[dense, :] = conductance * k
        return 0

    for part in range(2):
        landed(k_in, load_sem.at[part])
        lax.fori_loop(part * half, (part + 1) * half, prepare, 0)
    load_g.start()
    for i, src in enumerate(late):
        pltpu.make_async_copy(src, vec_f.at[1 + i], vec_sem.at[2]).start()

    n_face = cx * nb

    def face(y):
        return pl.ds(nb * yp + 8 + y, n_face, stride=yp)

    def dense_face(y):
        return pl.ds(y, n_face, stride=cy)

    y_of = (0, cy - 1)
    for side in range(2):
        first_y_send[side, 0] = root[face(y_of[side]), :]
        first_y_send[side, 1] = u_a[face(y_of[side]), :]
    for side in range(2):

        @pl.when(has_y[side])
        def _():
            y_copy(0, side).start()

    def around(ref, x, y0):
        here, sums = [], []
        for j in range(nb):
            at = ((x + 1) * nb + j) * yp + 8 + y0
            here.append(ref[at : at + CHUNK, :])
        for j in range(nb):
            at = ((x + 1) * nb + j) * yp + 8 + y0
            before = here[j - 1] if j > 0 else 0.0
            after = here[j + 1] if j < nb - 1 else 0.0
            left = pltpu.roll(jnp.where(lane == LANES - 1, before, here[j]), 1, 1)
            right = pltpu.roll(jnp.where(lane == 0, after, here[j]), LANES - 1, 1)
            step = nb * yp
            total = ref[at + step : at + step + CHUNK, :] + ref[at - step : at - step + CHUNK, :]
            total = total + (ref[at + 1 : at + 1 + CHUNK, :] + ref[at - 1 : at - 1 + CHUNK, :])
            sums.append(total + (left + right))
        return here, sums

    def sweep(turn, src, dst, planes, chunks):
        for x in planes:
            for c in chunks:
                y0 = c * CHUNK
                here, sums = around(src, x, y0)
                if turn == 0:
                    roots, root_sums = around(root, x, y0)
                for j in range(nb):
                    at = ((x + 1) * nb + j) * yp + 8 + y0
                    dense = (x * nb + j) * cy + y0
                    if turn == 0:
                        a = 1.0 - conductance * (roots[j] * root_sums[j])
                        coef_a[dense : dense + CHUNK, :] = a
                    else:
                        a = coef_a[dense : dense + CHUNK, :]
                    new = a * here[j] + coef_c[dense : dense + CHUNK, :] * sums[j]
                    if turn < SWEEPS - 1:
                        dst[at : at + CHUNK, :] = new
                    else:
                        out_v[x, y0 : y0 + CHUNK, j * LANES : (j + 1) * LANES] = (
                            new * inv[dense : dense + CHUNK, :]
                        )

    def fix_x(turn, side, c, src, dst):
        x = 0 if side == 0 else cx - 1
        y0 = c * CHUNK
        for j in range(nb):
            at = pl.ds(((x + 1) * nb + j) * yp + 8 + y0, CHUNK)
            dense = pl.ds((x * nb + j) * cy + y0, CHUNK)
            part = slice(j * CHUNK, (j + 1) * CHUNK)
            ys, zs = slice(y0, y0 + CHUNK), slice(j * LANES, (j + 1) * LANES)
            if turn == 0:
                k = first_x[side, 0, ys, zs]
                s = k * lax.rsqrt(k)
                halo = s * first_x[side, 1, ys, zs]
                less = conductance * (root[at, :] * s)
                coef_a[dense, :] = coef_a[dense, :] - less
                new = dst[at, :] + (coef_c[dense, :] * halo - less * src[at, :])
            else:
                halo = later_x[turn - 1, side, c, part, :]
                if turn < SWEEPS - 1:
                    new = dst[at, :] + coef_c[dense, :] * halo
            if turn < SWEEPS - 1:
                dst[at, :] = new
                later_x_send[turn, side, c, part, :] = new
            else:
                out_v[x, ys, zs] = out_v[x, ys, zs] + coef_c[dense, :] * inv[dense, :] * halo

    def take_x(turn, c, src, dst):
        for side in range(2):

            @pl.when(has_x[side])
            def _():
                if turn == 0:
                    landed(first_x.at[side, :, pl.ds(c * CHUNK, CHUNK)], fx_recv.at[side, c])
                else:
                    landed(later_x.at[turn - 1, side, c], lx_recv.at[turn - 1, side, c])
                fix_x(turn, side, c, src, dst)
                if turn < SWEEPS - 1:
                    later_x_copy(turn + 1, side, c).start()

    n_inner = (cx - 4) * nb

    def inner_face(y):
        return pl.ds(3 * nb * yp + 8 + y, n_inner, stride=yp)

    def inner_dense(y):
        return pl.ds(2 * nb * cy + y, n_inner, stride=cy)

    def corner_faces(y):
        for i, x in enumerate((0, cx - 2)):
            yield (
                pl.ds((x + 1) * nb * yp + 8 + y, 2 * nb, stride=yp),
                pl.ds(x * nb * cy + y, 2 * nb, stride=cy),
                slice(2 * i * nb, 2 * (i + 1) * nb),
            )

    def take_y(turn, src, dst):
        for side in range(2):

            @pl.when(has_y[side])
            def _():
                if turn == 0:
                    landed(first_y.at[side], y_recv.at[turn, side])
                    at, dense = face(y_of[side]), dense_face(y_of[side])
                    s, halo = first_y[side, 0], first_y[side, 1]
                    less = conductance * (root[at, :] * s)
                    coef_a[dense, :] = coef_a[dense, :] - less
                    dst[at, :] = dst[at, :] + (coef_c[dense, :] * halo - less * src[at, :])
                else:
                    landed(later_y.at[turn - 1, side], y_recv.at[turn, side])
                    if turn < SWEEPS - 1:
                        at, dense = inner_face(y_of[side]), inner_dense(y_of[side])
                        dst[at, :] = dst[at, :] + coef_c[dense, :] * later_y[turn - 1, side]
                    else:
                        src[inner_face(-1 if side == 0 else cy), :] = later_y[turn - 1, side]

    def take_corner(turn, src, dst):
        for side in range(2):

            @pl.when(has_y[side])
            def _():
                landed(corner.at[turn - 1, side], corner_recv.at[turn - 1, side])
                if turn < SWEEPS - 1:
                    for at, dense, part in corner_faces(y_of[side]):
                        dst[at, :] = dst[at, :] + coef_c[dense, :] * corner[turn - 1, side, part, :]
                else:
                    for at, _, part in corner_faces(-1 if side == 0 else cy):
                        src[at, :] = corner[turn - 1, side, part, :]

    def send_y(turn, ref):
        for side in range(2):

            @pl.when(has_y[side])
            def _():
                later_y_send[turn - 1, side] = ref[inner_face(y_of[side]), :]
                y_copy(turn, side).start()

    def send_corner(turn, ref):
        for side in range(2):

            @pl.when(has_y[side])
            def _():
                for at, _, part in corner_faces(y_of[side]):
                    corner_send[turn - 1, side, part, :] = ref[at, :]
                corner_copy(turn, side).start()

    every = list(range(n_ch))
    inner, outer = range(2, cx - 2), (0, 1, cx - 2, cx - 1)
    per = n_gx // n_gy
    home = gx // per
    share = gx % per

    def gather_copy():
        return remote(slip_send.at[0], slip_part.at[gy], gather_ssem, gather_rsem, gx, home)

    def gather_slip():
        @pl.when(home != gy)
        def _():
            gather_copy().start()

        @pl.when(home == gy)
        def _():
            slip_part[pl.ds(gy, 1)] = slip_send[...]

    def gather_when(mine):
        @pl.when(mine)
        def _():
            finish(1, 1)
            gather_slip()

    quarter = cx // 4
    late_x = (gx == n_gx // 2) | (gx == n_gx // 2 - 1)
    sweep(0, u_a, u_b, range(quarter), every)
    for axis in (1, 0):
        hear(axis, 0)
        tell(axis, 1)
    sweep(0, u_a, u_b, range(quarter, 2 * quarter), every)
    gather_when(gx == 0)
    if relayed:
        pass_on(0)
    sweep(0, u_a, u_b, range(2 * quarter, 3 * quarter), every)
    gather_when((gx > 0) & jnp.logical_not(late_x))
    for i in range(1, len(relayed)):
        pass_on(i)
    sweep(0, u_a, u_b, range(3 * quarter, cx), every)

    def req_copy(off):
        return remote(
            req_send.at[0], req_recv.at[gx], req_ssem, req_rsem, (gx + off) % n_gx, gy
        )


    def slip_copy(off):
        part = pl.ds(share * n_gy, n_gy)
        return remote(
            slip_part.at[pl.ds(0, n_gy)], slip_recv.at[part], slip_ssem, slip_rsem, (gx + off) % n_gx, gy
        )

    def spread_slip():
        @pl.when(home == gy)
        def _():
            landed(slip_part.at[pl.ds(0, n_gy - 1)], gather_rsem)
            for off in range(1, n_gx):
                slip_copy(off).start()
            slip_recv[pl.ds(share * n_gy, n_gy)] = slip_part[:n_gy]

    take_y(0, u_a, u_b)
    send_y(1, u_b)
    hear(0, 1)
    tell(0, 2)
    for c in edges:
        take_x(0, c, u_a, u_b)
    send_corner(1, u_b)
    gather_when((gx > 0) & late_x)
    sweep(1, u_b, u_a, inner, every)
    finish(0, 2)
    for off in range(1, n_gx):
        req_copy(off).start()

    def next_y(mine):
        @pl.when(mine)
        def _():
            take_y(1, u_b, u_a)
            send_y(2, u_a)

    next_y(late_x)
    for c in middles:
        take_x(0, c, u_a, u_b)
    spread_slip()
    sweep(1, u_b, u_a, outer, every)
    next_y(jnp.logical_not(late_x))

    take_corner(1, u_b, u_a)
    for c in edges:
        take_x(1, c, u_b, u_a)
    send_corner(2, u_a)
    if middles:
        sweep(2, u_a, None, inner, middles)

    landed(req_recv.at[pl.ds(0, n_gx - 1)], req_rsem)
    asked = pltpu.roll(req_recv[...], (width + (1 - gx) * cap) % width, 2)
    at_x, in_x = part_of(asked, cy * nz), rest_of(asked, cy * nz)
    at_y, at_z = part_of(in_x, nz), rest_of(in_x, nz)
    at_j, at_l = part_of(at_z, LANES), rest_of(at_z, LANES)
    slot_at = lax.broadcasted_iota(jnp.int32, asked.shape, 2)
    above, below = slot_at >= 2 * cap, slot_at < cap
    req_at[0] = ((at_x + 1) * nb + at_j) * yp + 8 + at_y
    req_at[1] = (at_x * nb + at_j) * cy + at_y
    req_at[2] = at_l
    req_at[3] = jnp.where(at_z == 0, -1, at_l + (LANES - 1))
    req_at[4] = jnp.where(at_z == nz - 1, -1, at_l - (LANES - 1))
    req_at[5] = (jnp.where(above, cx, 1) * nb + at_j) * yp + 8 + at_y
    req_at[6] = jnp.where((above & (at_x == 0)) | (below & (at_x == cx - 1)), at_l, -1)
    to_smem = pltpu.make_async_copy(req_at, req_smem, vec_sem.at[0])
    to_smem.start()

    landed(vec_f.at[pl.ds(1, len(late))], vec_sem.at[2])
    distance = vec_f[6]
    ratio = distance / vec_f[0]
    state_next = ratio + (vec_f[1] - ratio) * jnp.exp(-heal_time / ratio)
    state_ref[...] = state_next
    evolved = vec_f[5] * jnp.log(state_next / distance)

    @pl.when(home != gy)
    def _():
        landed(slip_recv.at[pl.ds(0, per * n_gy)], slip_rsem)

    if per > 1:

        @pl.when(home == gy)
        def _():
            landed(slip_recv.at[pl.ds(0, (per - 1) * n_gy)], slip_rsem)

    load_g.wait()
    n_cb = cols // LANES
    segment = [jnp.zeros((1, LANES), jnp.float32) for _ in range(n_cb)]
    for i in range(n_gx):
        first, shift = (i * tri) // LANES, (i * tri) % LANES
        row = slip_recv[i]
        if shift:
            row = pltpu.roll(row, shift, 1)
        segment[first] = segment[first] + jnp.where(lane >= shift, row, 0.0)
        if shift + tri > LANES:
            segment[first + 1] = segment[first + 1] + jnp.where(lane < shift, row, 0.0)
    eye_f = lax.broadcasted_iota(jnp.int32, (tri, LANES), 0) == lax.broadcasted_iota(
        jnp.int32, (tri, LANES), 1
    )
    for part in range(n_gy):
        for comp in range(2):
            total = jnp.zeros((tri, LANES), jnp.float32)
            for b in range(n_cb):
                block = g_in[comp, part * tri : (part + 1) * tri, b * LANES : (b + 1) * LANES]
                total = total + block * segment[b]
            sums = jnp.sum(total, axis=1, keepdims=True)
            part_send[part, comp : comp + 1, :] = jnp.sum(
                jnp.where(eye_f, sums, 0.0), axis=0, keepdims=True
            )

    def part_copy(off):
        to = (gy + off) % n_gy
        return remote(
            part_send.at[to], part_recv.at[gy], part_ssem, part_rsem, gx, to
        )

    part_recv[pl.ds(gy, 1)] = part_send[pl.ds(gy, 1)]
    for off in range(1, n_gy):
        part_copy(off).start()


    for c in middles:
        take_x(1, c, u_b, u_a)
    to_smem.wait()

    def across(source, _):
        for s in range(2 * cap):
            slot = s if s < cap else cap + s
            row = u_a[pl.ds(req_smem[5, source, 0, slot], 1), :]
            pick_c[source, s : s + 1, :] = jnp.where(
                lane == req_smem[6, source, 0, slot], row, 0.0
            )
        return 0

    lax.fori_loop(0, n_gx, across, 0)
    take_y(2, u_a, None)
    take_corner(2, u_a, None)

    def answer(source, _):
        for s in range(cap):
            slot = cap + s
            at = req_smem[0, source, 0, slot]
            dense = pl.ds(req_smem[1, source, 0, slot], 1)
            z = req_smem[2, source, 0, slot]
            here = u_a[pl.ds(at, 1), :]
            step = nb * yp
            beside = (u_a[pl.ds(at + step, 1), :] + u_a[pl.ds(at - step, 1), :]) + (
                u_a[pl.ds(at + 1, 1), :] + u_a[pl.ds(at - 1, 1), :]
            )
            near = jnp.where((lane == z - 1) | (lane == z + 1), here, 0.0)
            near = near + jnp.where(
                lane == req_smem[3, source, 0, slot], u_a[pl.ds(at - yp, 1), :], 0.0
            )
            near = near + jnp.where(
                lane == req_smem[4, source, 0, slot], u_a[pl.ds(at + yp, 1), :], 0.0
            )
            back = inv[dense, :]
            weight = coef_c[dense, :] * back
            pick_a[source, s : s + 1, :] = jnp.where(
                lane == z, (coef_a[dense, :] * here) * back + weight * beside, 0.0
            )
            pick_b[source, s : s + 1, :] = jnp.where(lane == z, weight, 0.0)
            pick_n[source, s : s + 1, :] = near
        return 0

    lax.fori_loop(0, n_gx, answer, 0)

    def spread(values, first):
        n = values.shape[1]
        to_lane = lax.broadcasted_iota(jnp.int32, (n_gx, n, width), 2)
        of_slot = lax.broadcasted_iota(jnp.int32, (n_gx, n, width), 1)
        return jnp.sum(jnp.where(to_lane == first(of_slot), values, 0.0), axis=1, keepdims=True)

    def own(slot):
        return jnp.where(slot < cap, gx * cap + slot, -1)

    def beyond(slot):
        lane_of = jnp.where(slot < cap, (gx - 1) * cap + slot, gx * cap + slot)
        return jnp.where(slot < 2 * cap, lane_of, -1)

    weights = jnp.sum(pick_b[...], axis=2, keepdims=True)
    values = jnp.sum(pick_a[...], axis=2, keepdims=True) + weights * jnp.sum(
        pick_n[...], axis=2, keepdims=True
    )
    ans_send[:, 0] = spread(values, own)
    ans_send[:, 1] = spread(weights, own)
    ans_send[:, 2] = spread(jnp.sum(pick_c[...], axis=2, keepdims=True), beyond)

    def ans_copy(off):
        to = (gx + off) % n_gx
        return remote(
            ans_send.at[to], ans_recv.at[gx], ans_ssem, ans_rsem, to, gy
        )

    for off in range(1, n_gx):
        ans_copy(off).start()
    ans_recv[pl.ds(gx, 1)] = ans_send[pl.ds(gx, 1)]

    sweep(2, u_a, None, inner, edges)
    sweep(2, u_a, None, outer, every)
    for c in edges + middles:
        take_x(2, c, u_a, None)

    landed(ans_recv.at[pl.ds(0, n_gx - 1)], ans_rsem)
    answers = [ans_recv[0, i] for i in range(3)]
    for other in range(1, n_gx):
        answers = [answers[i] + ans_recv[other, i] for i in range(3)]
    answers = answers[0] + answers[1] * answers[2]
    found = jnp.sum(jnp.where(slot_col == slot_lane, answers, 0.0), axis=1, keepdims=True)
    fault = jnp.sum(jnp.where(eye, found, 0.0), axis=0, keepdims=True)
    landed(part_recv.at[pl.ds(0, n_gy - 1)], part_rsem)
    rates = part_recv[0]
    for other in range(1, n_gy):
        rates = rates + part_recv[other]
    shear = vec_f[3] + step_time * rates[0:1, :tri]
    loaded = vec_f[2] + step_time * rates[1:2, :tri]
    log_ref[...] = (shear / (loaded - fault) - friction_ref - evolved) / vec_f[4]

    for side in range(2):

        @pl.when(has_x[side])
        def _():
            landed(p_in.at[pl.ds(0, SWEEPS + 1)], x_send.at[side])

        @pl.when(has_y[side])
        def _():
            landed(coef_a.at[pl.ds(0, (SWEEPS + 1) * n_face)], y_send.at[side])

        if relayed:

            @pl.when(is_end[side])
            def _():
                landed(relay_x.at[pl.ds(0, len(relayed))], relay_send)

    @pl.when(home != gy)
    def _():
        gather_copy().wait_send()

    @pl.when(home == gy)
    def _():
        landed(slip_part, slip_ssem)

    landed(req_recv.at[pl.ds(0, n_gx - 1)], req_ssem)
    landed(ans_recv.at[pl.ds(0, n_gx - 1)], ans_ssem)
    landed(part_recv.at[pl.ds(0, n_gy - 1)], part_ssem)


def part_of(value, size):
    if size & (size - 1) == 0:
        return lax.shift_right_logical(value, jnp.int32(size.bit_length() - 1))
    return lax.div(value, jnp.int32(size))


def rest_of(value, size):
    if size & (size - 1) == 0:
        return value & (size - 1)
    return lax.rem(value, jnp.int32(size))


def write_kernel(p_ref, state_in, log_in, out_hbm, state_hbm, log_hbm, sem):
    planes = p_ref.shape[0]
    n = 4 if planes % 4 == 0 else 1
    small = [
        pltpu.make_async_copy(state_in, state_hbm, sem.at[1]),
        pltpu.make_async_copy(log_in, log_hbm, sem.at[2]),
    ]
    for copy in small:
        copy.start()
    for i in range(n):
        part = pl.ds(i * planes // n, planes // n)
        pltpu.make_async_copy(p_ref.at[part], out_hbm.at[part], sem.at[0]).start()
    pltpu.make_async_copy(p_ref, out_hbm, sem.at[0]).wait()
    for copy in small:
        copy.wait()


def local(
    pressure,
    permeability,
    kernel,
    slip_rate,
    aging_state,
    normal_stress,
    shear_stress,
    direct_effect,
    evolution_effect,
    slip_distance,
    tri_owner,
    tri_cell,
):
    n_gx, n_gy = lax.axis_size("gx"), lax.axis_size("gy")
    cx, cy, nz = pressure.shape
    tri = slip_rate.shape[0]
    _, rows, cols = kernel.shape
    cap = max(2, 2 * tri // n_gx)
    cap_pad = -(-cap // 8) * 8
    nb = nz // LANES
    yp = cy + 8
    n_ch = cy // CHUNK
    padded = ((cx + 2) * nb * yp + 8, LANES)
    dense = (cx * nb * cy, LANES)
    width = -(-n_gx * cap // LANES) * LANES
    dims = (n_gx, n_gy, cx, cy, nz, tri, rows, cols, cap, cap_pad)
    f32, i32 = jnp.float32, jnp.int32
    dma = pltpu.SemaphoreType.DMA
    hbm = lambda a: pltpu.with_memory_space_constraint(a, pltpu.HBM)
    vec = lambda a: hbm(a.reshape(1, tri))
    any_spec = pl.BlockSpec(memory_space=pl.ANY)
    hbm_spec = pl.BlockSpec(memory_space=pltpu.HBM)
    vmem_spec = pl.BlockSpec(memory_space=pltpu.VMEM)
    out, state, log = pl.pallas_call(
        functools.partial(step_kernel, dims),
        out_shape=(
            pltpu.VMEM(pressure.shape, f32),
            pltpu.VMEM((1, tri), f32),
            pltpu.VMEM((1, tri), f32),
        ),
        in_specs=[hbm_spec] * 12,
        out_specs=(vmem_spec, vmem_spec, vmem_spec),
        scratch_shapes=[
            pltpu.VMEM(pressure.shape, f32),
            pltpu.VMEM(pressure.shape, f32),
            pltpu.VMEM(kernel.shape, f32),
            pltpu.VMEM((7, 1, tri), f32),
            pltpu.VMEM((2, 1, tri), i32),
            pltpu.VMEM(padded, f32),
            pltpu.VMEM(padded, f32),
            pltpu.VMEM(padded, f32),
            pltpu.VMEM(dense, f32),
            pltpu.VMEM(dense, f32),
            pltpu.VMEM(dense, f32),
            pltpu.VMEM((2, 2, cy, nz), f32),
            pltpu.VMEM((2, 2, CHUNK, nz), f32),
            pltpu.VMEM((SWEEPS - 1, 2, n_ch, nb * CHUNK, LANES), f32),
            pltpu.VMEM((SWEEPS - 1, 2, n_ch, nb * CHUNK, LANES), f32),
            pltpu.VMEM((2, 2, cx * nb, LANES), f32),
            pltpu.VMEM((2, 2, cx * nb, LANES), f32),
            pltpu.VMEM((SWEEPS - 1, 2, (cx - 4) * nb, LANES), f32),
            pltpu.VMEM((SWEEPS - 1, 2, (cx - 4) * nb, LANES), f32),
            pltpu.VMEM((SWEEPS - 1, 2, 4 * nb, LANES), f32),
            pltpu.VMEM((SWEEPS - 1, 2, 4 * nb, LANES), f32),
            pltpu.VMEM((1, 1, LANES), f32),
            pltpu.VMEM((n_gy * (n_gx - 1), 1, LANES), f32),
            pltpu.VMEM((n_gx, 1, LANES), f32),
            pltpu.VMEM((1, 1, width), i32),
            pltpu.VMEM((n_gx, 1, width), i32),
            pltpu.VMEM((7, n_gx, 1, width), i32),
            pltpu.SMEM((7, n_gx, 1, width), i32),
            pltpu.VMEM((n_gy, 2, LANES), f32),
            pltpu.VMEM((n_gy, 2, LANES), f32),
            pltpu.VMEM((n_gx, cap_pad, LANES), f32),
            pltpu.VMEM((n_gx, cap_pad, LANES), f32),
            pltpu.VMEM((n_gx, cap_pad, LANES), f32),
            pltpu.VMEM((n_gx, -(-2 * cap // 8) * 8, LANES), f32),
            pltpu.VMEM((n_gx, 3, 1, width), f32),
            pltpu.VMEM((n_gx, 3, 1, width), f32),
            dma((2,)),
            dma((4,)),
            dma((2,)),
            dma((2, n_ch)),
            dma((SWEEPS - 1, 2, n_ch)),
            dma,
            dma((2,)),
            dma((2,)),
            dma((SWEEPS, 2)),
            dma((SWEEPS - 1, 2)),
            pltpu.SemaphoreType.REGULAR((max(1, (n_gx - 2).bit_length()),)),
            pltpu.SemaphoreType.REGULAR((max(1, (n_gy - 2).bit_length()),)),
            dma,
            dma,
            dma,
            dma,
            dma,
            dma,
            dma,
            dma,
            dma,
            dma,
        ],
        compiler_params=pltpu.CompilerParams(
            collective_id=0, has_side_effects=True, vmem_limit_bytes=40 << 20
        ),
        name="fault_step",
    )(
        hbm(pressure),
        hbm(permeability),
        hbm(kernel),
        vec(slip_rate),
        vec(aging_state),
        vec(normal_stress),
        vec(shear_stress),
        vec(direct_effect),
        vec(evolution_effect),
        vec(slip_distance),
        vec(tri_owner),
        vec(tri_cell),
    )
    out, state, log = pl.pallas_call(
        write_kernel,
        out_shape=(
            jax.ShapeDtypeStruct(pressure.shape, f32),
            jax.ShapeDtypeStruct((1, tri), f32),
            jax.ShapeDtypeStruct((1, tri), f32),
        ),
        in_specs=[vmem_spec] * 3,
        out_specs=(any_spec,) * 3,
        scratch_shapes=[dma((3,))],
        compiler_params=pltpu.CompilerParams(vmem_limit_bytes=4 << 20),
        name="write_out",
    )(out, state, log)
    return out, state.reshape(tri), log.reshape(tri)


def solution(mesh):
    fault = P(("gx", "gy"))
    field = P("gx", "gy", None)
    in_specs = (field, field, P(None, "gx", "gy")) + (fault,) * 7 + (P(("gx", "gy"), None), fault)
    out_specs = (field, fault, fault)
    return jax.shard_map(local, mesh=mesh, in_specs=in_specs, out_specs=out_specs, check_vma=False)
```
